128 devices in a mesh: rows: 16 (over z, x), cols: 8 (over y, core).
Axes of the slice: x: 4, y: 4, z: 4, core: 2. Of those that a mesh axis runs over, the one named last changes fastest.
Arguments:
- points: float32 [160, 127], replicated, may hold values from -0.5 to 0.5
- noise: float32 [160, 128], replicated, may hold values from 0.3 to 3
- basis: float32 [20480, 128], P('rows'), may hold values from -0.5 to 0.5
Outputs:
- factor: float32 [20480, 20480], P('rows', 'cols')
The draws below stay inside these ranges and needn't reach their ends.
All inputs are finite; a program needn't handle non-finite values.
Results may differ from the reference program's by a relative error of at most 0.0003.
Values sent between devices are 32-bit elements; how exact they have to be, the bound alone decides.
A program may use at most 128 MiB of HBM per device.

```python
import math
import jax
import jax.numpy as jnp
from jax import lax

D = 127
W = 128
NB = 128
NPT = 160
PW = 256
PANELS = 2
ORDER = 20480
LEAD = 512


def shard_levels(key, shape, shards, smallest, high):
    gain, own = 1.0, jax.random.fold_in(key, 6)
    for axis_at, blocks in shards:
        draws = jnp.exp(jax.random.uniform(jax.random.fold_in(own, axis_at), (blocks,), jnp.float32, smallest / len(shards), high / len(shards)))
        gain = gain * jnp.repeat(draws, shape[axis_at] // blocks).reshape([-1 if axis == axis_at else 1 for axis in range(len(shape))])
    return gain


def gaussian(rng, shape, spread, bound, shards=(), kind=jnp.bfloat16):
    result = spread * jax.random.normal(rng, shape, jnp.float32)
    if shards:
        result = result * shard_levels(rng, shape, shards, -0.22, 0.18)
    return jnp.clip(result, -bound, bound).astype(kind)


def setup_inputs(seed: int = 0) -> dict:
    seeds = jax.random.split(jax.random.key(seed), 4)
    return {
        "points": gaussian(seeds[0], (NPT, D), D ** -0.5, 0.5, (), jnp.float32),
        "noise": jnp.clip(jnp.exp(jax.random.uniform(seeds[1], (NPT, W), jnp.float32, math.log(0.3), math.log(3.0))), 0.3, 3.0),
        "basis": gaussian(seeds[2], (ORDER, NB), NB ** -0.5, 0.5, ((0, 16),), jnp.float32),
    }


def tile_rows(point_row, col_points):
    rho = point_row[None, :] - col_points
    kval = jnp.exp(-0.5 * jnp.sum(rho * rho, axis=1))
    ones = jnp.ones((col_points.shape[0], 1), jnp.float32)
    left = jnp.concatenate([ones, -rho], axis=1)
    right = jnp.concatenate([ones, rho], axis=1)
    width = left.shape[1]
    jmat = jnp.diag((jnp.arange(width) > 0).astype(jnp.float32))
    tiles = kval[None, :, None] * (jmat[:, None, :] + left.T[:, :, None] * right[None, :, :])
    return tiles.reshape(width, -1)

def point_rows(point_row, noise_row, basis_row, start, col_points, col_basis, col_start):
    width = noise_row.shape[0]
    values = tile_rows(point_row, col_points) + jnp.dot(basis_row, col_basis.T, precision=lax.Precision.HIGHEST)
    row_ids = start + jnp.arange(width).astype(jnp.int32)
    col_ids = col_start + jnp.arange(values.shape[1]).astype(jnp.int32)
    same = row_ids[:, None] == col_ids[None, :]
    return values + jnp.where(same, noise_row[:, None], jnp.float32(0.0))

def assemble(points_rows, noise_rows, basis_rows, starts, col_points, col_basis, col_start):
    count, width = noise_rows.shape
    basis_split = basis_rows.reshape(count, width, -1)

    def single(items):
        return point_rows(items[0], items[1], items[2], items[3], col_points, col_basis, col_start)
    blocks = lax.map(single, (points_rows, noise_rows, basis_split, starts))
    return blocks.reshape(count * width, -1)

def factor_panels(columns, row_ids, panel_width, panels):
    lead = None
    for panel_index in range(panels):
        low = panel_index * panel_width
        block = columns[:, low:low + panel_width]
        if lead is not None:
            block = block - jnp.dot(lead, lead[low:low + panel_width].T, precision=lax.Precision.HIGHEST)
        diag = jnp.linalg.cholesky(block[low:low + panel_width])
        panel = lax.linalg.triangular_solve(diag, block, left_side=False, lower=True, transpose_a=True)
        col_ids = low + jnp.arange(panel_width).astype(jnp.int32)
        panel = jnp.where(row_ids[:, None] < col_ids[None, :], jnp.float32(0.0), panel)
        lead = panel if lead is None else jnp.concatenate([lead, panel], axis=1)
    return lead

def finish(points_rows, noise_rows, basis_rows, starts, lead_rows, col_points, col_basis, col_start, lead_cols):
    count, width = noise_rows.shape
    ncols = lead_cols.shape[0]
    leading = lead_rows.shape[1]
    cross = lead_cols.T
    col_ids = col_start + jnp.arange(ncols).astype(jnp.int32)

    def single(items):
        prow, nrow, brow, lrow, start = items
        values = point_rows(prow, nrow, brow, start, col_points, col_basis, col_start)
        trail = values - jnp.dot(lrow, cross, precision=lax.Precision.HIGHEST)
        row_ids = start + jnp.arange(width).astype(jnp.int32)
        own = jnp.pad(lrow, ((0, 0), (0, ncols - leading)))
        mirror = lax.dynamic_slice_in_dim(cross, jnp.minimum(start, leading - width).astype(jnp.int32), width, 0)
        inner = jnp.where(row_ids[:, None] < leading, mirror, trail)
        return jnp.where(col_ids[None, :] < leading, own, inner)
    blocks = lax.map(single, (points_rows, noise_rows, basis_rows.reshape(count, width, -1), lead_rows.reshape(count, width, leading), starts))
    return blocks.reshape(count * width, ncols)

def reference(points, noise, basis):
    count, width = noise.shape
    order = count * width
    lead_points = LEAD // width
    starts = (width * jnp.arange(count)).astype(jnp.int32)
    columns = assemble(points, noise, basis, starts, points[:lead_points], basis[:LEAD], 0)
    row_ids = jnp.arange(order).astype(jnp.int32)
    lead = factor_panels(columns, row_ids, PW, PANELS)
    return finish(points, noise, basis, starts, lead, points, basis, 0, lead)
```

```python
import jax
import jax.numpy as jnp
from jax import lax
from jax.experimental import pallas as pl
from jax.experimental.pallas import tpu as pltpu
from jax.sharding import PartitionSpec as P

W = 128
LEAD = 512
NL = LEAD // W
NR = 10
NC = 20
RG = 16
PIECE = LEAD // RG
MESH = pl.DeviceIdType.MESH
HI = lax.Precision.HIGHEST
F32 = jnp.float32
BF = jnp.bfloat16


def dot(a, b):
    return lax.dot_general(a, b, (((1,), (0,)), ((), ())), precision=HI, preferred_element_type=F32)


def dot_nt(a, b):
    return lax.dot_general(a, b, (((1,), (1,)), ((), ())), precision=HI, preferred_element_type=F32)


def dot_tn(a, b):
    return lax.dot_general(a, b, (((0,), (0,)), ((), ())), precision=HI, preferred_element_type=F32)


def split(x):
    high = x.astype(BF)
    return high, (x - high.astype(F32)).astype(BF)


def spread_kernel(basis_ref, lead_ref, send_a, send_b, recv, local):
    r = lax.axis_index("rows")
    c = lax.axis_index("cols")
    barrier = pltpu.get_barrier_semaphore()
    for off in range(1, RG):
        pl.semaphore_signal(barrier, inc=1, device_id=(lax.rem(r + off, RG), c), device_id_type=MESH)
    pl.semaphore_wait(barrier, RG - 1)

    def first(t):
        rows = pl.ds(PIECE * t, PIECE)
        return pltpu.make_async_remote_copy(
            src_ref=basis_ref.at[rows], dst_ref=lead_ref.at[rows], send_sem=send_a.at[t], recv_sem=recv.at[t],
            device_id=(t, c), device_id_type=MESH)

    def zero(t):
        rows = pl.ds(0, PIECE)
        return pltpu.make_async_remote_copy(
            src_ref=basis_ref.at[rows], dst_ref=lead_ref.at[rows], send_sem=send_b.at[t], recv_sem=recv.at[0],
            device_id=(t, c), device_id_type=MESH)

    def second(off):
        rows = pl.ds(pl.multiple_of(PIECE * r, PIECE), PIECE)
        return pltpu.make_async_remote_copy(
            src_ref=lead_ref.at[rows], dst_ref=lead_ref.at[rows], send_sem=send_b.at[off], recv_sem=recv.at[r],
            device_id=(lax.rem(r + off, RG), c), device_id_type=MESH)

    @pl.when(r == 0)
    def _():
        for t in range(1, RG):
            first(t).start()
        for t in range(1, RG):
            zero(t).start()
        own = pltpu.make_async_copy(basis_ref.at[pl.ds(0, LEAD)], lead_ref, local)
        own.start()
        own.wait()
        for t in range(1, RG):
            first(t).wait_send()
            zero(t).wait_send()

    @pl.when(r != 0)
    def _():
        rows = pl.ds(pl.multiple_of(PIECE * r, PIECE), PIECE)
        pltpu.make_async_remote_copy(
            src_ref=lead_ref.at[rows], dst_ref=lead_ref.at[rows], send_sem=send_a.at[0], recv_sem=recv.at[r],
            device_id=(0, c), device_id_type=MESH).wait_recv()
        for off in range(1, RG):
            @pl.when(r + off != RG)
            def _():
                second(off).start()
        for off in range(1, RG):
            q = lax.rem(r + off, RG)
            rows_q = pl.ds(pl.multiple_of(PIECE * q, PIECE), PIECE)
            pltpu.make_async_remote_copy(
                src_ref=lead_ref.at[rows_q], dst_ref=lead_ref.at[rows_q], send_sem=send_a.at[0], recv_sem=recv.at[q],
                device_id=(0, c), device_id_type=MESH).wait_recv()
        for off in range(1, RG):
            @pl.when(r + off != RG)
            def _():
                second(off).wait_send()


def spread(basis):
    return pl.pallas_call(
        spread_kernel,
        out_shape=jax.ShapeDtypeStruct((LEAD, W), F32),
        in_specs=[pl.BlockSpec(memory_space=pl.ANY)],
        out_specs=pl.BlockSpec(memory_space=pltpu.VMEM),
        scratch_shapes=[
            pltpu.SemaphoreType.DMA((RG,)),
            pltpu.SemaphoreType.DMA((RG,)),
            pltpu.SemaphoreType.DMA((RG,)),
            pltpu.SemaphoreType.DMA,
        ],
        compiler_params=pltpu.CompilerParams(collective_id=0, has_side_effects=True),
    )(basis)


def eye_masks():
    row = lax.broadcasted_iota(jnp.int32, (W, W), 0)
    col = lax.broadcasted_iota(jnp.int32, (W, W), 1)
    same = row == col
    return same, same & (col > 0)


def unit_row():
    return (lax.broadcasted_iota(jnp.int32, (1, W), 1) == 0).astype(F32)


def unit_col():
    return (lax.broadcasted_iota(jnp.int32, (W, 1), 0) == 0).astype(F32)


def kval(a_row, b_row):
    rho = a_row - b_row
    return jnp.exp(-0.5 * jnp.sum(rho * rho, axis=1, keepdims=True))


def tile(k, a_row, b_row, a_col, b_col, jmask):
    p = k * (unit_col() + b_col - a_col)
    q = unit_row() + a_row - b_row
    return jnp.where(jmask, k, 0.0) + p * q


def lane_splat(v, j):
    return jnp.broadcast_to(v[:, j:j + 1], (8, W))


def row_splat(v, j):
    return jnp.broadcast_to(v[j:j + 1, :], (8, W))


def invert_block(read, write):
    n = W // 8
    lane = lax.broadcasted_iota(jnp.int32, (8, W), 1)
    sub = lax.broadcasted_iota(jnp.int32, (8, W), 0)
    rows = {}

    def take(r):
        return rows.pop(r) if r in rows else read(r)

    for k in range(n):
        own = (lane >= 8 * k) & (lane < 8 * k + 8)
        top = take(k)
        cols = [lane_splat(top, 8 * k + j) for j in range(8)]
        if k + 1 < n:
            following = take(k + 1)
            ahead = [lane_splat(following, 8 * k + j) for j in range(8)]
        q = jnp.where(own, (lane - 8 * k == sub).astype(F32), top)
        w = None
        for j in range(8):
            d = row_splat(cols[j], j)
            inv = 1.0 / d
            row_j = row_splat(q, j)
            w_j = row_j * lax.rsqrt(d)
            w = w_j if w is None else jnp.where(sub == j, w_j, w)
            m = jnp.where(sub == j, 1.0 - inv, cols[j] * inv)
            for j2 in range(j + 1, 8):
                cols[j2] = cols[j2] - m * row_splat(cols[j2], j)
            q = q - m * row_j
        write(k, jnp.where(lane <= 8 * k + sub, w, 0.0))
        if k + 1 < n:
            qs = [row_splat(q, j) for j in range(8)]

            def update(v, c):
                t0 = c[0] * qs[0] + c[1] * qs[1]
                t1 = c[2] * qs[2] + c[3] * qs[3]
                t2 = c[4] * qs[4] + c[5] * qs[5]
                t3 = c[6] * qs[6] + c[7] * qs[7]
                return jnp.where(own, 0.0, v) - ((t0 + t1) + (t2 + t3))

            rows[k + 1] = update(following, ahead)
            for r in range(k + 2, n):
                v = take(r)
                rows[r] = update(v, [lane_splat(v, 8 * k + j) for j in range(8)])


def lead_kernel(points_ref, noise_ref, lead_ref, m_ref, g_ref, work, square):
    same, jmask = eye_masks()
    square[...] = jnp.zeros((W, W), F32)
    square[0:8, :] = points_ref[0:8, :]
    turned = square[...].T
    work[...] = dot_nt(lead_ref[...], lead_ref[...])
    for i in range(NL):
        for j in range(NL):
            a_row, b_row = points_ref[i:i + 1, :], points_ref[j:j + 1, :]
            t = tile(kval(a_row, b_row), a_row, b_row, turned[:, i:i + 1], turned[:, j:j + 1], jmask)
            if i == j:
                t = t + jnp.where(same, noise_ref[i:i + 1, :], 0.0)
            work[W * i:W * i + W, W * j:W * j + W] += t
    for p in range(NL):
        lo, hi = W * p, W * p + W

        def write(k, v):
            m_ref[lo + 8 * k:lo + 8 * k + 8, lo:hi] = v

        invert_block(lambda k: work[lo + 8 * k:lo + 8 * k + 8, lo:hi], write)
        inv = m_ref[lo:hi, lo:hi]
        if p:
            m_ref[lo:hi, 0:lo] = dot(inv, work[lo:hi, 0:lo])
        if hi < LEAD:
            m_ref[lo:hi, hi:] = jnp.zeros((W, LEAD - hi), F32)
            u = dot(inv, work[lo:hi, hi:])
            work[hi:, hi:] -= dot_tn(u, u)
            e = dot_tn(u, m_ref[lo:hi, 0:hi])
            if p:
                work[hi:, 0:lo] -= e[:, 0:lo]
            work[hi:, lo:hi] = -e[:, lo:hi]
    g_ref[...] = dot_tn(m_ref[...], m_ref[...])


def lead_inverse(points, noise, lead):
    return pl.pallas_call(
        lead_kernel,
        out_shape=(jax.ShapeDtypeStruct((LEAD, LEAD), F32), jax.ShapeDtypeStruct((LEAD, LEAD), F32)),
        scratch_shapes=[pltpu.VMEM((LEAD, LEAD), F32), pltpu.VMEM((W, W), F32)],
        compiler_params=pltpu.CompilerParams(vmem_limit_bytes=40 << 20),
        cost_estimate=pl.CostEstimate(flops=4 * 10 ** 10, bytes_accessed=4 * 10 ** 6, transcendentals=512),
    )(points, noise, lead)


ROWS_AT, COLS_AT = 8, 32


def finish_kernel(pos, points_ref, noise_ref, basis_ref, lead_ref, m_ref, g_ref, cols0_ref, cols1_ref, out_ref,
                  square, turned, own, h, lhs, panel, kp, coef, kij, rhs):
    r, c, x = pos()
    step = pl.program_id(0)
    same, jmask = eye_masks()
    lane = lax.broadcasted_iota(jnp.int32, (W, W), 1)
    row_idx = lax.broadcasted_iota(jnp.int32, (W, W), 0)

    @pl.when(step == 0)
    def _():
        square[...] = jnp.zeros((W, W), F32)
        square[0:8, :] = points_ref[0:8, :]
        square[ROWS_AT:ROWS_AT + 16, :] = points_ref[pl.ds(NR * r, 16), :]
        square[COLS_AT:COLS_AT + 24, :] = points_ref[pl.ds(NC * c, 24), :]
        t = square[...].T
        turned[...] = t
        colp = square[COLS_AT:COLS_AT + 24, :]
        coef[...] = jnp.zeros((W, LEAD), F32)
        for m in range(NL):
            km = kval(colp, square[m:m + 1, :])
            kij[24 * m:24 * m + 24, :] = jnp.broadcast_to(km, (24, W))
            q = -km * (unit_row() + colp - square[m:m + 1, :])
            coef[0:NC, W * m:W * m + W] = q[0:NC, :]
            coef[NC + NC * m:2 * NC + NC * m, W * m:W * m + W] = q[0:NC, :]
        own[...] = dot_nt(basis_ref[...], lead_ref[...])
        tc = pltpu.roll(t, W - COLS_AT, 1)
        for i in range(NR):
            a_row = square[ROWS_AT + i:ROWS_AT + i + 1, :]
            a_col = t[:, ROWS_AT + i:ROWS_AT + i + 1]
            rows = slice(W * i, W * i + W)
            for l in range(NL):
                b_row = square[l:l + 1, :]
                v = tile(kval(a_row, b_row), a_row, b_row, a_col, t[:, l:l + 1], jmask)
                if i < NL and l == i:
                    v = v + jnp.where(same & (r == 0), noise_ref[l:l + 1, :], 0.0)
                own[rows, W * l:W * l + W] += v
            rho = tc - a_col
            kk = jnp.exp(-0.5 * jnp.sum(rho * rho, axis=0, keepdims=True))
            kij[96 + i:97 + i, :] = kk
            kp[rows, :] = jnp.where(lane < NC, kk * (unit_col() + rho), 0.0)
        for s in range(5):
            rows = slice(256 * s, 256 * s + 256)
            a = own[rows, :]
            hs = dot(a, g_ref[...])
            h[rows, :] = hs
            e = dot_nt(hs, coef[...]) + kp[rows, :]
            b = basis_ref[rows, :] - dot(hs, lead_ref[...])
            eh, el = split(e)
            bh, bl = split(b)
            lhs[rows, 0:128] = bh
            lhs[rows, 128:256] = bh
            lhs[rows, 256:384] = bl
            lhs[rows, 384:512] = eh
            lhs[rows, 512:640] = eh
            lhs[rows, 640:768] = el

        @pl.when(c == 0)
        def _():
            for s in range(5):
                rows = slice(256 * s, 256 * s + 256)
                v = dot_nt(own[rows, :], m_ref[...])
                rid = 256 * s + lax.broadcasted_iota(jnp.int32, (256, LEAD), 0)
                cid = lax.broadcasted_iota(jnp.int32, (256, LEAD), 1)
                panel[rows, :] = jnp.where((r == 0) & (rid < cid), 0.0, v)

    is_panel = (c == 0) & (step < 2)

    @pl.when(is_panel)
    def _():
        out_ref[...] = panel[:, pl.ds(pl.multiple_of(256 * jnp.minimum(step, 1), 256), 256)]

    @pl.when(jnp.logical_not(is_panel))
    def _():
        local = pl.ds(pl.multiple_of(256 * lax.rem(step, 5), 256), 256)
        flip = (x + step // 5) % 2 == 1
        b = jnp.where(flip, cols1_ref[local, :], cols0_ref[local, :])
        bh, bl = split(b)
        rhs[:, 0:128] = bh
        rhs[:, 128:256] = bl
        rhs[:, 256:384] = bh
        for s in range(2):
            j = 2 * step + s
            rows = slice(W * s, W * s + W)
            y = square[pl.ds(COLS_AT + j, 1), :]
            ycol = jnp.sum(jnp.where(same, y, 0.0), axis=1, keepdims=True)
            v = jnp.where(lane == j, unit_col() - ycol, 0.0)
            for m in range(NL):
                v = v + jnp.where(lane == NC + NC * m + j, turned[:, m:m + 1], 0.0)
            vh, vl = split(v)
            rhs[rows, 384:512] = vh
            rhs[rows, 512:640] = vl
            rhs[rows, 640:768] = vh

        def rows_pair(s, carry):
            base = pl.multiple_of(256 * s, 256)
            acc = lax.dot_general(lhs[pl.ds(base, 256), :], rhs[...], (((1,), (1,)), ((), ())), preferred_element_type=F32)
            for ii in range(2):
                i = 2 * s + ii
                at = pl.ds(pl.multiple_of(base + W * ii, W), W)
                y_i = square[pl.ds(ROWS_AT + i, 1), :]
                hi_m = [h[at, W * m:W * m + W] for m in range(NL)]
                kpi = kp[at, :]
                for jj in range(2):
                    j = 2 * step + jj
                    kcol = jnp.sum(jnp.where(lane == j, kpi, 0.0), axis=1, keepdims=True)
                    kk = jnp.sum(jnp.where(lane[0:1] == j, kij[pl.ds(96 + i, 1), :], 0.0), axis=1, keepdims=True)
                    v = acc[W * ii:W * ii + W, W * jj:W * jj + W] + kcol * y_i
                    comb = kij[pl.ds(j, 1), :] * hi_m[0]
                    for m in range(1, NL):
                        comb = comb + kij[pl.ds(24 * m + j, 1), :] * hi_m[m]
                    v = v - jnp.where(lane > 0, comb, 0.0) + jnp.where(jmask, kk, 0.0)
                    out_ref[at, W * jj:W * jj + W] = v

                    @pl.when(NR * r + i == NC * c + j)
                    def _():
                        out_ref[at, W * jj:W * jj + W] += jnp.where(same, noise_ref[pl.ds(NR * r + i, 1), :], 0.0)
            return carry

        lax.fori_loop(0, 5, rows_pair, 0)

        @pl.when(r == 0)
        def _():
            cross = dot_nt(lead_ref[...], b)
            for s in range(2):
                j = 2 * step + s
                b_row = square[pl.ds(COLS_AT + j, 1), :]
                b_col = jnp.sum(jnp.where(same, b_row, 0.0), axis=1, keepdims=True)
                for l in range(NL):
                    a_row = square[l:l + 1, :]
                    v = tile(kval(a_row, b_row), a_row, b_row, turned[:, l:l + 1], b_col, jmask)
                    own[W * l:W * l + W, W * s:W * s + W] = cross[W * l:W * l + W, W * s:W * s + W] + v
            out_ref[0:LEAD, :] = dot(m_ref[...], own[0:LEAD, 0:256])


def finish_call(pos, points, noise, basis, lead, m, g, cols0, cols1):
    rows = NR * W
    full = pl.BlockSpec(memory_space=pltpu.VMEM)
    return pl.pallas_call(
        lambda *refs: finish_kernel(pos, *refs),
        grid=(NC // 2,),
        out_shape=jax.ShapeDtypeStruct((rows, NC * W), F32),
        in_specs=[full] * 8,
        out_specs=pl.BlockSpec((rows, 2 * W), lambda s: (0, s)),
        scratch_shapes=[
            pltpu.VMEM((W, W), F32),
            pltpu.VMEM((W, W), F32),
            pltpu.VMEM((rows, LEAD), F32),
            pltpu.VMEM((rows, LEAD), F32),
            pltpu.VMEM((rows, 6 * W), BF),
            pltpu.VMEM((rows, LEAD), F32),
            pltpu.VMEM((rows, W), F32),
            pltpu.VMEM((W, LEAD), F32),
            pltpu.VMEM((112, W), F32),
            pltpu.VMEM((2 * W, 6 * W), BF),
        ],
        compiler_params=pltpu.CompilerParams(vmem_limit_bytes=52 << 20),
    )(points, noise, basis, lead, m, g, cols0, cols1)


def permute_pairs(t):
    pairs = []
    for z in range(4):
        for x in range(4):
            for y in range(4):
                for k in range(2):
                    source = (4 * y + 2 * k + (t + x) % 2) * 8 + ((2 * y + 2 - z) % 4) * 2 + x // 2
                    pairs.append((source, (4 * z + x) * 8 + 2 * y + k))
    return pairs


def body(points, noise, basis):
    points = jnp.pad(points, ((0, 32), (1, 0)))
    cols0 = lax.ppermute(basis, ("rows", "cols"), permute_pairs(0))
    cols1 = lax.ppermute(basis, ("rows", "cols"), permute_pairs(1))
    lead = spread(basis)
    m, g = lead_inverse(points, noise, lead)

    def pos():
        r = lax.axis_index("rows")
        return r, lax.axis_index("cols"), lax.rem(r, 4)

    return finish_call(pos, points, noise, basis, lead, m, g, cols0, cols1)


def solution(mesh):
    placed = (P(), P(), P("rows", None))
    return jax.shard_map(body, mesh=mesh, in_specs=placed, out_specs=P("rows", "cols"), check_vma=False)
```

```python
import jax
import jax.numpy as jnp
from jax import lax
from jax.experimental import pallas as pl
from jax.experimental.pallas import tpu as pltpu
from jax.sharding import PartitionSpec as P

W = 128
LEAD = 512
NL = LEAD // W
NR = 10
NC = 20
RG = 16
HALF = LEAD // 2
PIECE = HALF // RG
BLOCK_HALF = NR * W // 2
CHUNKS = 4
CHUNK = BLOCK_HALF // CHUNKS
MESH = pl.DeviceIdType.MESH
HI = lax.Precision.HIGHEST
F32 = jnp.float32
BF = jnp.bfloat16


def dot(a, b):
    return lax.dot_general(a, b, (((1,), (0,)), ((), ())), precision=HI, preferred_element_type=F32)


def dot_nt(a, b):
    return lax.dot_general(a, b, (((1,), (1,)), ((), ())), precision=HI, preferred_element_type=F32)


def dot_tn(a, b):
    return lax.dot_general(a, b, (((0,), (0,)), ((), ())), precision=HI, preferred_element_type=F32)


def split(x):
    high = x.astype(BF)
    return high, (x - high.astype(F32)).astype(BF)


class Moves:
    def __init__(self, basis, lead, stage, cols, sems):
        self.basis, self.lead, self.stage, self.cols = basis, lead, stage, cols
        (self.first_sem, self.second_sem, self.lead_recv, self.half_sem, self.local_sem,
         self.a_send, self.a_recv, self.b_send, self.b_recv) = sems
        self.r = lax.axis_index("rows")
        self.c = lax.axis_index("cols")
        self.z, self.x = self.r // 4, self.r % 4
        self.y, self.k = self.c // 2, self.c % 2
        self.home = self.x // 2

    def barrier(self):
        sem = pltpu.get_barrier_semaphore()
        for off in range(1, RG):
            pl.semaphore_signal(sem, inc=1, device_id=((self.r + off) % RG, self.c), device_id_type=MESH)
        for x in range(4):
            pl.semaphore_signal(sem, inc=1, device_id=(4 * self.z + x, 2 * self.y + 1 - self.k), device_id_type=MESH)
        pl.semaphore_wait(sem, RG + 3)

    def piece(self, source, q, send_sem, target):
        rows = pl.ds(pl.multiple_of(HALF * self.k + PIECE * q, PIECE), PIECE)
        return pltpu.make_async_remote_copy(
            src_ref=source.at[rows], dst_ref=self.lead.at[rows], send_sem=send_sem, recv_sem=self.lead_recv.at[q],
            device_id=(target, self.c), device_id_type=MESH)

    def exchange(self, core):
        rows = pl.ds(pl.multiple_of(HALF * core, HALF), HALF)
        return pltpu.make_async_remote_copy(
            src_ref=self.lead.at[rows], dst_ref=self.lead.at[rows], send_sem=self.half_sem.at[0], recv_sem=self.half_sem.at[1],
            device_id=(self.r, 2 * self.y + 1 - self.k), device_id_type=MESH)

    def spread_lead(self):
        r = self.r

        @pl.when(r == 0)
        def _():
            for t in range(1, RG):
                self.piece(self.basis, t, self.first_sem.at[t], t).start()
            for t in range(1, RG):
                self.piece(self.basis, 0, self.second_sem.at[t], t).start()
            own = pltpu.make_async_copy(self.basis.at[pl.ds(0, LEAD)], self.lead, self.local_sem.at[0])
            own.start()
            own.wait()
            for t in range(1, RG):
                self.piece(self.basis, t, self.first_sem.at[t], t).wait_send()
                self.piece(self.basis, 0, self.second_sem.at[t], t).wait_send()

        @pl.when(r != 0)
        def _():
            self.piece(self.lead, r, self.first_sem.at[0], 0).wait_recv()
            for off in range(1, RG):
                @pl.when(r + off != RG)
                def _():
                    self.piece(self.lead, r, self.second_sem.at[off], (r + off) % RG).start()
            for off in range(1, RG):
                self.piece(self.lead, (r + off) % RG, self.first_sem.at[0], 0).wait_recv()
            self.exchange(self.k).start()
            self.exchange(1 - self.k).wait_recv()
            self.exchange(self.k).wait_send()
            for off in range(1, RG):
                @pl.when(r + off != RG)
                def _():
                    self.piece(self.lead, r, self.second_sem.at[off], (r + off) % RG).wait_send()

    def own_rows(self, n):
        return pl.ds(pl.multiple_of(BLOCK_HALF * self.k + CHUNK * n, CHUNK), CHUNK)

    def along_z(self, n, dz):
        return pltpu.make_async_remote_copy(
            src_ref=self.basis.at[self.own_rows(n)], dst_ref=self.stage.at[pl.ds(CHUNK * n, CHUNK)],
            send_sem=self.a_send.at[n, dz], recv_sem=self.a_recv.at[n],
            device_id=(4 * ((self.z + dz) % 4) + self.x, self.c), device_id_type=MESH)

    def keep(self, n):
        return pltpu.make_async_copy(self.basis.at[self.own_rows(n)], self.stage.at[pl.ds(CHUNK * n, CHUNK)], self.local_sem.at[1 + n])

    def start_z(self):
        @pl.when(self.z == self.y)
        def _():
            for n in range(CHUNKS):
                for dz in (1, 3, 2):
                    self.along_z(n, dz).start()
                self.keep(n).start()

    def place(self, block, half, n):
        return pl.ds(pl.multiple_of(2 * BLOCK_HALF * block + BLOCK_HALF * half + CHUNK * n, CHUNK), CHUNK)

    def along_x(self, n, dx):
        return pltpu.make_async_remote_copy(
            src_ref=self.stage.at[pl.ds(CHUNK * n, CHUNK)], dst_ref=self.cols.at[self.place(self.x % 2, self.k, n)],
            send_sem=self.b_send.at[n, dx], recv_sem=self.b_recv.at[self.x % 2, self.k, n],
            device_id=(4 * self.z + (self.x + dx) % 4, 2 * self.y + self.home), device_id_type=MESH)

    def settle(self, n):
        return pltpu.make_async_copy(self.stage.at[pl.ds(CHUNK * n, CHUNK)], self.cols.at[self.place(self.x % 2, self.k, n)], self.local_sem.at[1 + CHUNKS + n])

    def forward(self, n):
        @pl.when(self.z == self.y)
        def _():
            self.keep(n).wait()

        @pl.when(self.z != self.y)
        def _():
            self.along_z(n, 1).wait_recv()

        for dx in (1, 3, 2):
            self.along_x(n, dx).start()

        @pl.when(self.home == self.k)
        def _():
            self.settle(n).start()

        @pl.when(self.home != self.k)
        def _():
            self.along_x(n, 0).start()

    def finish(self):
        for n in range(CHUNKS):
            for block in range(2):
                for half in range(2):
                    mine = (self.home == self.k) & (self.x % 2 == block) & (self.k == half)

                    @pl.when(jnp.logical_not(mine))
                    def _():
                        rows = self.place(block, half, n)
                        pltpu.make_async_remote_copy(
                            src_ref=self.cols.at[rows], dst_ref=self.cols.at[rows], send_sem=self.b_send.at[n, 0],
                            recv_sem=self.b_recv.at[block, half, n],
                            device_id=(self.r, 2 * self.y + 1 - self.k), device_id_type=MESH).wait_recv()
        for n in range(CHUNKS):
            for dx in (1, 3, 2):
                self.along_x(n, dx).wait_send()

            @pl.when(self.home == self.k)
            def _():
                self.settle(n).wait()

            @pl.when(self.home != self.k)
            def _():
                self.along_x(n, 0).wait_send()

            @pl.when(self.z == self.y)
            def _():
                for dz in (1, 3, 2):
                    self.along_z(n, dz).wait_send()


def eye_masks():
    row = lax.broadcasted_iota(jnp.int32, (W, W), 0)
    col = lax.broadcasted_iota(jnp.int32, (W, W), 1)
    same = row == col
    return same, same & (col > 0)


def unit_row():
    return (lax.broadcasted_iota(jnp.int32, (1, W), 1) == 0).astype(F32)


def unit_col():
    return (lax.broadcasted_iota(jnp.int32, (W, 1), 0) == 0).astype(F32)


def kval(a_row, b_row):
    rho = a_row - b_row
    return jnp.exp(-0.5 * jnp.sum(rho * rho, axis=1, keepdims=True))


def tile(k, a_row, b_row, a_col, b_col, jmask):
    p = k * (unit_col() + b_col - a_col)
    q = unit_row() + a_row - b_row
    return jnp.where(jmask, k, 0.0) + p * q


def lane_splat(v, j):
    return jnp.broadcast_to(v[:, j:j + 1], (8, W))


def row_splat(v, j):
    return jnp.broadcast_to(v[j:j + 1, :], (8, W))


def invert_block(read, write):
    n = W // 8
    lane = lax.broadcasted_iota(jnp.int32, (8, W), 1)
    sub = lax.broadcasted_iota(jnp.int32, (8, W), 0)
    rows = {}

    def take(r):
        return rows.pop(r) if r in rows else read(r)

    for k in range(n):
        own = (lane >= 8 * k) & (lane < 8 * k + 8)
        top = take(k)
        cols = [lane_splat(top, 8 * k + j) for j in range(8)]
        if k + 1 < n:
            following = take(k + 1)
            ahead = [lane_splat(following, 8 * k + j) for j in range(8)]
        q = jnp.where(own, (lane - 8 * k == sub).astype(F32), top)
        w = None
        for j in range(8):
            d = row_splat(cols[j], j)
            inv = 1.0 / d
            row_j = row_splat(q, j)
            w_j = row_j * lax.rsqrt(d)
            w = w_j if w is None else jnp.where(sub == j, w_j, w)
            m = jnp.where(sub == j, 1.0 - inv, cols[j] * inv)
            for j2 in range(j + 1, 8):
                cols[j2] = cols[j2] - m * row_splat(cols[j2], j)
            q = q - m * row_j
        write(k, jnp.where(lane <= 8 * k + sub, w, 0.0))
        if k + 1 < n:
            qs = [row_splat(q, j) for j in range(8)]

            def update(v, c):
                t0 = c[0] * qs[0] + c[1] * qs[1]
                t1 = c[2] * qs[2] + c[3] * qs[3]
                t2 = c[4] * qs[4] + c[5] * qs[5]
                t3 = c[6] * qs[6] + c[7] * qs[7]
                return jnp.where(own, 0.0, v) - ((t0 + t1) + (t2 + t3))

            rows[k + 1] = update(following, ahead)
            for r in range(k + 2, n):
                v = take(r)
                rows[r] = update(v, [lane_splat(v, 8 * k + j) for j in range(8)])


def lead_kernel(points_ref, noise_ref, basis_ref, lead_ref, cols_ref, m_ref, g_ref, work, square, stage, *sems):
    moves = Moves(basis_ref, lead_ref, stage, cols_ref, sems)
    moves.barrier()
    moves.spread_lead()
    moves.start_z()

    def after(p):
        if p < 2:
            for n in range(CHUNKS // 2):
                moves.forward(CHUNKS // 2 * p + n)

    factor(points_ref, noise_ref, lead_ref, m_ref, g_ref, work, square, after)
    moves.finish()


def factor(points_ref, noise_ref, lead_ref, m_ref, g_ref, work, square, after):
    same, jmask = eye_masks()
    square[...] = jnp.zeros((W, W), F32)
    square[0:8, :] = points_ref[0:8, :]
    turned = square[...].T
    work[...] = dot_nt(lead_ref[...], lead_ref[...])
    for i in range(NL):
        for j in range(NL):
            a_row, b_row = points_ref[i:i + 1, :], points_ref[j:j + 1, :]
            t = tile(kval(a_row, b_row), a_row, b_row, turned[:, i:i + 1], turned[:, j:j + 1], jmask)
            if i == j:
                t = t + jnp.where(same, noise_ref[i:i + 1, :], 0.0)
            work[W * i:W * i + W, W * j:W * j + W] += t
    for p in range(NL):
        lo, hi = W * p, W * p + W

        def write(k, v):
            m_ref[lo + 8 * k:lo + 8 * k + 8, lo:hi] = v

        invert_block(lambda k: work[lo + 8 * k:lo + 8 * k + 8, lo:hi], write)
        inv = m_ref[lo:hi, lo:hi]
        if p:
            m_ref[lo:hi, 0:lo] = dot(inv, work[lo:hi, 0:lo])
        if hi < LEAD:
            m_ref[lo:hi, hi:] = jnp.zeros((W, LEAD - hi), F32)
            u = dot(inv, work[lo:hi, hi:])
            work[hi:, hi:] -= dot_tn(u, u)
            e = dot_tn(u, m_ref[lo:hi, 0:hi])
            if p:
                work[hi:, 0:lo] -= e[:, 0:lo]
            work[hi:, lo:hi] = -e[:, lo:hi]
        after(p)
    g_ref[...] = dot_tn(m_ref[...], m_ref[...])


def lead_inverse(points, noise, basis):
    vmem = pl.BlockSpec(memory_space=pltpu.VMEM)
    dma = pltpu.SemaphoreType.DMA
    return pl.pallas_call(
        lead_kernel,
        out_shape=(
            jax.ShapeDtypeStruct((LEAD, W), F32),
            jax.ShapeDtypeStruct((NC * W, W), F32),
            jax.ShapeDtypeStruct((LEAD, LEAD), F32),
            jax.ShapeDtypeStruct((LEAD, LEAD), F32),
        ),
        in_specs=[vmem, vmem, pl.BlockSpec(memory_space=pl.ANY)],
        out_specs=(vmem,) * 4,
        scratch_shapes=[
            pltpu.VMEM((LEAD, LEAD), F32),
            pltpu.VMEM((W, W), F32),
            pltpu.VMEM((BLOCK_HALF, W), F32),
            dma((RG,)),
            dma((RG,)),
            dma((RG,)),
            dma((2,)),
            dma((1 + 2 * CHUNKS,)),
            dma((CHUNKS, 4)),
            dma((CHUNKS,)),
            dma((CHUNKS, 4)),
            dma((2, 2, CHUNKS)),
        ],
        compiler_params=pltpu.CompilerParams(collective_id=0, has_side_effects=True, vmem_limit_bytes=24 << 20),
        cost_estimate=pl.CostEstimate(flops=4 * 10 ** 10, bytes_accessed=4 * 10 ** 6, transcendentals=512),
    )(points, noise, basis)


def factor_only(points, noise, lead):
    return pl.pallas_call(
        lambda p, n, l, m, g, work, square: factor(p, n, l, m, g, work, square, lambda q: None),
        out_shape=(jax.ShapeDtypeStruct((LEAD, LEAD), F32), jax.ShapeDtypeStruct((LEAD, LEAD), F32)),
        scratch_shapes=[pltpu.VMEM((LEAD, LEAD), F32), pltpu.VMEM((W, W), F32)],
        compiler_params=pltpu.CompilerParams(vmem_limit_bytes=24 << 20),
    )(points, noise, lead)


ROWS_AT, COLS_AT = 8, 32
NT = NL + NR


def three_left(x):
    high, low = split(x)
    return jnp.concatenate([high, high, low], axis=1)


def three_right(x, axis):
    high, low = split(x)
    return jnp.concatenate([high, low, high], axis=axis)


def bdot(a, b):
    return lax.dot_general(a, b, (((1,), (0,)), ((), ())), preferred_element_type=F32)


def bdot_nt(a, b):
    return lax.dot_general(a, b, (((1,), (1,)), ((), ())), preferred_element_type=F32)


def finish_kernel(pos, points_ref, noise_ref, basis_ref, lead_ref, m_ref, g_ref, cols_ref, out_ref,
                  square, turned, own, h, lhs, panel, kp, table, rhs, g3, f3, m3):
    r, c = pos()
    step = pl.program_id(0)
    same, jmask = eye_masks()
    lane = lax.broadcasted_iota(jnp.int32, (W, W), 1)

    @pl.when(step == 0)
    def _():
        square[...] = jnp.zeros((W, W), F32)
        square[0:8, :] = points_ref[0:8, :]
        square[ROWS_AT:ROWS_AT + 16, :] = points_ref[pl.ds(NR * r, 16), :]
        square[COLS_AT:COLS_AT + 24, :] = points_ref[pl.ds(NC * c, 24), :]
        t = square[...].T
        turned[...] = t
        colp = square[COLS_AT:COLS_AT + 24, :]
        coef = []
        total = []
        for m in range(NL):
            km = kval(colp, square[m:m + 1, :])
            table[m, :, :] = jnp.broadcast_to(km, (24, W))
            q = (-km * (unit_row() + colp - square[m:m + 1, :]))[0:24]
            total.append(q)
            pieces = [q if n == m else jnp.zeros((24, W), F32) for n in range(NL)]
            coef.append(jnp.concatenate(pieces, axis=1))
        weights = jnp.concatenate([jnp.concatenate(total, axis=1)] + coef + [jnp.zeros((W - 24 * (NL + 1), LEAD), F32)], axis=0)
        f3[0:W, :] = three_right(weights, 1)
        f3[W:2 * W, :] = three_right(lead_ref[...].T, 1)
        g3[...] = three_right(g_ref[...], 0)
        b3 = three_left(basis_ref[...])
        l3 = three_right(lead_ref[...], 1)
        own[...] = bdot_nt(b3, l3)
        tc = pltpu.roll(t, W - COLS_AT, 1)
        for i in range(NR):
            a_row = square[ROWS_AT + i:ROWS_AT + i + 1, :]
            a_col = t[:, ROWS_AT + i:ROWS_AT + i + 1]
            rows = slice(W * i, W * i + W)
            for l in range(NL):
                b_row = square[l:l + 1, :]
                v = tile(kval(a_row, b_row), a_row, b_row, a_col, t[:, l:l + 1], jmask)
                if l == i:
                    v = v + jnp.where(same & (r == 0), noise_ref[l:l + 1, :], 0.0)
                own[rows, W * l:W * l + W] += v
            rho = tc - a_col
            kk = jnp.exp(-0.5 * jnp.sum(rho * rho, axis=0, keepdims=True))
            kp[rows, :] = jnp.where(lane < NC, kk * (unit_col() + rho), 0.0)
            table[NL + i, :, :] = jnp.broadcast_to(kval(colp, a_row), (24, W))
            h[rows, LEAD:LEAD + W] = jnp.where(jmask, -1.0, 0.0) + a_col * a_row
        for s in range(5):
            rows = slice(256 * s, 256 * s + 256)
            hs = bdot(three_left(own[rows, :]), g3[...])
            for m in range(NL):
                h[rows, W * m:W * m + W] = jnp.where(lax.broadcasted_iota(jnp.int32, (256, W), 1) > 0, hs[:, W * m:W * m + W], 0.0)
            eb = bdot_nt(three_left(hs), f3[...])
            lhs[rows, 0:3 * W] = three_left(basis_ref[rows, :] - eb[:, W:])
            lhs[rows, 3 * W:] = three_left(eb[:, 0:W] + kp[rows, :])

        @pl.when((c == 0) | (r == 0))
        def _():
            m3[...] = three_left(m_ref[...])

        @pl.when(c == 0)
        def _():
            for s in range(5):
                rows = slice(256 * s, 256 * s + 256)
                v = bdot_nt(three_right(own[rows, :], 1), m3[...])
                rid = 256 * s + lax.broadcasted_iota(jnp.int32, (256, LEAD), 0)
                cid = lax.broadcasted_iota(jnp.int32, (256, LEAD), 1)
                panel[rows, :] = jnp.where((r == 0) & (rid < cid), 0.0, v)

    is_panel = (c == 0) & (step < 2)

    @pl.when(is_panel)
    def _():
        out_ref[...] = panel[:, pl.ds(pl.multiple_of(256 * jnp.minimum(step, 1), 256), 256)]

    @pl.when(jnp.logical_not(is_panel))
    def _():
        b = cols_ref[pl.ds(pl.multiple_of(256 * step, 256), 256), :]
        rhs[:, 0:3 * W] = three_right(b, 1)
        bases = []
        for s in range(2):
            j = 2 * step + s
            y = square[pl.ds(COLS_AT + j, 1), :]
            ycol = jnp.sum(jnp.where(same, y, 0.0), axis=1, keepdims=True)
            bases.append(jnp.broadcast_to(unit_col() + ycol, (W, W)))
            v = jnp.where(lane == j, unit_col() - ycol, 0.0)
            for m in range(NL):
                v = v + jnp.where(lane == 24 + 24 * m + j, turned[:, m:m + 1], 0.0)
            rhs[W * s:W * s + W, 3 * W:] = three_right(v, 1)

        def rows_block(s):
            rows = slice(256 * s, 256 * s + 256)
            acc = bdot_nt(lhs[rows, :], rhs[...])
            for ii in range(2):
                i = 2 * s + ii
                at = slice(W * i, W * i + W)
                y_i = square[ROWS_AT + i:ROWS_AT + i + 1, :]
                his = [h[at, W * m:W * m + W] for m in range(NL + 1)]
                for jj in range(2):
                    ks = [table[m, pl.ds(2 * step + jj, 1), :] for m in range(NL)]
                    ks.append(table[NL + i, pl.ds(2 * step + jj, 1), :])
                    v = acc[W * ii:W * ii + W, W * jj:W * jj + W] + bases[jj] * (ks[NL] * y_i)
                    comb = (ks[0] * his[0] + ks[1] * his[1]) + (ks[2] * his[2] + ks[3] * his[3])
                    out_ref[at, W * jj:W * jj + W] = v - (comb + ks[4] * his[4])

        @pl.when(r == 0)
        def _():
            cross = bdot_nt(three_left(lead_ref[...]), rhs[:, 0:3 * W])
            for s in range(2):
                b_row = square[pl.ds(COLS_AT + 2 * step + s, 1), :]
                b_col = bases[s][:, 0:1] - unit_col()
                for l in range(NL):
                    a_row = square[l:l + 1, :]
                    v = tile(kval(a_row, b_row), a_row, b_row, turned[:, l:l + 1], b_col, jmask)
                    own[W * l:W * l + W, W * s:W * s + W] = cross[W * l:W * l + W, W * s:W * s + W] + v
            out_ref[0:LEAD, :] = bdot(m3[...], three_right(own[0:LEAD, 0:256], 0))
            for s in range(2, 5):
                rows_block(s)

        @pl.when(r != 0)
        def _():
            for s in range(5):
                rows_block(s)

        for s in range(2):
            i = NC * c + 2 * step + s - NR * r

            @pl.when((i >= 0) & (i < NR) & ((r > 0) | (i >= NL)))
            def _():
                at = pl.ds(pl.multiple_of(W * i, W), W)
                out_ref[at, W * s:W * s + W] += jnp.where(same, noise_ref[pl.ds(NR * r + i, 1), :], 0.0)


def finish_call(pos, points, noise, basis, lead, m, g, cols):
    rows = NR * W
    full = pl.BlockSpec(memory_space=pltpu.VMEM)
    return pl.pallas_call(
        lambda *refs: finish_kernel(pos, *refs),
        grid=(NC // 2,),
        out_shape=jax.ShapeDtypeStruct((rows, NC * W), F32),
        in_specs=[full] * 7,
        out_specs=pl.BlockSpec((rows, 2 * W), lambda s: (0, s)),
        scratch_shapes=[
            pltpu.VMEM((W, W), F32),
            pltpu.VMEM((W, W), F32),
            pltpu.VMEM((rows, LEAD), F32),
            pltpu.VMEM((rows, LEAD + W), F32),
            pltpu.VMEM((rows, 6 * W), BF),
            pltpu.VMEM((rows, LEAD), F32),
            pltpu.VMEM((rows, W), F32),
            pltpu.VMEM((NT, 24, W), F32),
            pltpu.VMEM((2 * W, 6 * W), BF),
            pltpu.VMEM((3 * LEAD, LEAD), BF),
            pltpu.VMEM((2 * W, 3 * LEAD), BF),
            pltpu.VMEM((LEAD, 3 * LEAD), BF),
        ],
        compiler_params=pltpu.CompilerParams(vmem_limit_bytes=40 << 20),
    )(points, noise, basis, lead, m, g, cols)


def body(points, noise, basis):
    points = jnp.pad(points, ((0, 32), (1, 0)))
    lead, cols, m, g = lead_inverse(points, noise, basis)

    def pos():
        return lax.axis_index("rows"), lax.axis_index("cols")

    return finish_call(pos, points, noise, basis, lead, m, g, cols)


def solution(mesh):
    placed = (P(), P(), P("rows", None))
    return jax.shard_map(body, mesh=mesh, in_specs=placed, out_specs=P("rows", "cols"), check_vma=False)
```

```python
from types import SimpleNamespace

import jax
import jax.numpy as jnp
from jax import lax
from jax.experimental import pallas as pl
from jax.experimental.pallas import tpu as pltpu
from jax.sharding import PartitionSpec as P

W = 128
LEAD = 512
NL = LEAD // W
NR = 10
NC = 20
RG = 16
HALF = LEAD // 2
PIECE = HALF // RG
BLOCK_HALF = NR * W // 2
CHUNKS = 4
CHUNK = BLOCK_HALF // CHUNKS
MESH = pl.DeviceIdType.MESH
HI = lax.Precision.HIGHEST
F32 = jnp.float32
BF = jnp.bfloat16


def dot(a, b):
    return lax.dot_general(a, b, (((1,), (0,)), ((), ())), precision=HI, preferred_element_type=F32)


def dot_nt(a, b):
    return lax.dot_general(a, b, (((1,), (1,)), ((), ())), precision=HI, preferred_element_type=F32)


def dot_tn(a, b):
    return lax.dot_general(a, b, (((0,), (0,)), ((), ())), precision=HI, preferred_element_type=F32)


def split(x):
    high = x.astype(BF)
    return high, (x - high.astype(F32)).astype(BF)


class Moves:
    def __init__(self, basis, lead, stage, cols, sems):
        self.basis, self.lead, self.stage, self.cols = basis, lead, stage, cols
        (self.first_sem, self.second_sem, self.lead_recv, self.half_sem, self.local_sem,
         self.a_send, self.a_recv, self.b_send, self.b_recv) = sems
        self.r = lax.axis_index("rows")
        self.c = lax.axis_index("cols")
        self.z, self.x = self.r // 4, self.r % 4
        self.y, self.k = self.c // 2, self.c % 2
        self.home = self.x // 2

    def barrier(self):
        sem = pltpu.get_barrier_semaphore()
        for off in range(1, RG):
            pl.semaphore_signal(sem, inc=1, device_id=((self.r + off) % RG, self.c), device_id_type=MESH)
        for x in range(4):
            pl.semaphore_signal(sem, inc=1, device_id=(4 * self.z + x, 2 * self.y + 1 - self.k), device_id_type=MESH)
        pl.semaphore_wait(sem, RG + 3)

    def piece(self, source, q, send_sem, target):
        rows = pl.ds(pl.multiple_of(HALF * self.k + PIECE * q, PIECE), PIECE)
        return pltpu.make_async_remote_copy(
            src_ref=source.at[rows], dst_ref=self.lead.at[rows], send_sem=send_sem, recv_sem=self.lead_recv.at[q],
            device_id=(target, self.c), device_id_type=MESH)

    def exchange(self, core):
        rows = pl.ds(pl.multiple_of(HALF * core, HALF), HALF)
        return pltpu.make_async_remote_copy(
            src_ref=self.lead.at[rows], dst_ref=self.lead.at[rows], send_sem=self.half_sem.at[0], recv_sem=self.half_sem.at[1],
            device_id=(self.r, 2 * self.y + 1 - self.k), device_id_type=MESH)

    def start_spread(self):
        @pl.when(self.r == 0)
        def _():
            for t in range(1, RG):
                self.piece(self.basis, t, self.first_sem.at[t], t).start()
            for t in range(1, RG):
                self.piece(self.basis, 0, self.second_sem.at[t], t).start()
            pltpu.make_async_copy(self.basis.at[pl.ds(0, LEAD)], self.lead, self.local_sem.at[0]).start()

        @pl.when(self.r != 0)
        def _():
            self.piece(self.lead, self.r, self.first_sem.at[0], 0).wait_recv()
            for off in range(1, RG):
                @pl.when(self.r + off != RG)
                def _():
                    self.piece(self.lead, self.r, self.second_sem.at[off], (self.r + off) % RG).start()

    def finish_spread(self):
        @pl.when(self.r == 0)
        def _():
            pltpu.make_async_copy(self.basis.at[pl.ds(0, LEAD)], self.lead, self.local_sem.at[0]).wait()
            for t in range(1, RG):
                self.piece(self.basis, t, self.first_sem.at[t], t).wait_send()
                self.piece(self.basis, 0, self.second_sem.at[t], t).wait_send()

        @pl.when(self.r != 0)
        def _():
            for off in range(1, RG):
                self.piece(self.lead, (self.r + off) % RG, self.first_sem.at[0], 0).wait_recv()
            self.exchange(self.k).start()
            self.exchange(1 - self.k).wait_recv()
            self.exchange(self.k).wait_send()
            for off in range(1, RG):
                @pl.when(self.r + off != RG)
                def _():
                    self.piece(self.lead, self.r, self.second_sem.at[off], (self.r + off) % RG).wait_send()

    def own_rows(self, n):
        return pl.ds(pl.multiple_of(BLOCK_HALF * self.k + CHUNK * n, CHUNK), CHUNK)

    def along_z(self, n, dz):
        return pltpu.make_async_remote_copy(
            src_ref=self.basis.at[self.own_rows(n)], dst_ref=self.stage.at[pl.ds(CHUNK * n, CHUNK)],
            send_sem=self.a_send.at[n, dz], recv_sem=self.a_recv.at[n],
            device_id=(4 * ((self.z + dz) % 4) + self.x, self.c), device_id_type=MESH)

    def keep(self, n):
        return pltpu.make_async_copy(self.basis.at[self.own_rows(n)], self.stage.at[pl.ds(CHUNK * n, CHUNK)], self.local_sem.at[1 + n])

    def start_z(self):
        @pl.when(self.z == self.y)
        def _():
            for n in range(CHUNKS):
                for dz in (1, 3, 2):
                    self.along_z(n, dz).start()
                self.keep(n).start()

    def place(self, block, half, n):
        return pl.ds(pl.multiple_of(2 * BLOCK_HALF * block + BLOCK_HALF * half + CHUNK * n, CHUNK), CHUNK)

    def along_x(self, n, dx):
        return pltpu.make_async_remote_copy(
            src_ref=self.stage.at[pl.ds(CHUNK * n, CHUNK)], dst_ref=self.cols.at[self.place(self.x % 2, self.k, n)],
            send_sem=self.b_send.at[n, dx], recv_sem=self.b_recv.at[self.x % 2, self.k, n],
            device_id=(4 * self.z + (self.x + dx) % 4, 2 * self.y + self.home), device_id_type=MESH)

    def settle(self, n):
        return pltpu.make_async_copy(self.stage.at[pl.ds(CHUNK * n, CHUNK)], self.cols.at[self.place(self.x % 2, self.k, n)], self.local_sem.at[1 + CHUNKS + n])

    def forward(self, n):
        @pl.when(self.z == self.y)
        def _():
            self.keep(n).wait()

        @pl.when(self.z != self.y)
        def _():
            self.along_z(n, 1).wait_recv()

        for dx in (1, 3, 2):
            self.along_x(n, dx).start()

        @pl.when(self.home == self.k)
        def _():
            self.settle(n).start()

        @pl.when(self.home != self.k)
        def _():
            self.along_x(n, 0).start()

    def finish(self):
        for n in range(CHUNKS):
            for block in range(2):
                for half in range(2):
                    mine = (self.home == self.k) & (self.x % 2 == block) & (self.k == half)

                    @pl.when(jnp.logical_not(mine))
                    def _():
                        rows = self.place(block, half, n)
                        pltpu.make_async_remote_copy(
                            src_ref=self.cols.at[rows], dst_ref=self.cols.at[rows], send_sem=self.b_send.at[n, 0],
                            recv_sem=self.b_recv.at[block, half, n],
                            device_id=(self.r, 2 * self.y + 1 - self.k), device_id_type=MESH).wait_recv()
        for n in range(CHUNKS):
            for dx in (1, 3, 2):
                self.along_x(n, dx).wait_send()

            @pl.when(self.home == self.k)
            def _():
                self.settle(n).wait()

            @pl.when(self.home != self.k)
            def _():
                self.along_x(n, 0).wait_send()

            @pl.when(self.z == self.y)
            def _():
                for dz in (1, 3, 2):
                    self.along_z(n, dz).wait_send()


def eye_masks():
    row = lax.broadcasted_iota(jnp.int32, (W, W), 0)
    col = lax.broadcasted_iota(jnp.int32, (W, W), 1)
    same = row == col
    return same, same & (col > 0)


def unit_row():
    return (lax.broadcasted_iota(jnp.int32, (1, W), 1) == 0).astype(F32)


def unit_col():
    return (lax.broadcasted_iota(jnp.int32, (W, 1), 0) == 0).astype(F32)


def kval(a_row, b_row):
    rho = a_row - b_row
    return jnp.exp(-0.5 * jnp.sum(rho * rho, axis=1, keepdims=True))


def tile(k, a_row, b_row, a_col, b_col, jmask):
    p = k * (unit_col() + b_col - a_col)
    q = unit_row() + a_row - b_row
    return jnp.where(jmask, k, 0.0) + p * q


def lane_splat(v, j):
    return jnp.broadcast_to(v[:, j:j + 1], (8, W))


def row_splat(v, j):
    return jnp.broadcast_to(v[j:j + 1, :], (8, W))


def invert_block(read, write):
    n = W // 8
    lane = lax.broadcasted_iota(jnp.int32, (8, W), 1)
    sub = lax.broadcasted_iota(jnp.int32, (8, W), 0)
    rows = {}

    def take(r):
        return rows[r] if r in rows else read(r)

    cols = [lane_splat(take(0), j) for j in range(8)]
    for k in range(n):
        own = (lane >= 8 * k) & (lane < 8 * k + 8)
        last = k + 1 == n
        if not last:
            following = take(k + 1)
            ahead = [lane_splat(following, 8 * k + j) for j in range(8)]
            below = list(ahead)
            later = [lane_splat(following, 8 * k + 8 + j) for j in range(8)]
        q = jnp.where(own, (lane - 8 * k == sub).astype(F32), take(k))
        w = scale = None
        for j in range(8):
            d = row_splat(cols[j], j)
            inv = 1.0 / d
            row_j = row_splat(q, j)
            others = jnp.where(sub == j, 0.0, cols[j])
            pivots = {j2: row_splat(cols[j2], j) for j2 in range(j + 1, 8)}
            for j2 in range(j + 1, 8):
                cols[j2] = cols[j2] - inv * (others * pivots[j2])
            q = q - inv * (others * row_j)
            w_j = row_j * lax.rsqrt(d)
            w = w_j if w is None else jnp.where(sub == j, w_j, w)
            scale = inv if scale is None else jnp.where(sub == j, inv, scale)
            if not last:
                m = below[j] * inv
                for j2 in range(j + 1, 8):
                    below[j2] = below[j2] - m * pivots[j2]
                for j2 in range(8):
                    later[j2] = later[j2] - m * row_splat(below[j], j2)
        write(k, jnp.where(lane <= 8 * k + sub, w, 0.0))
        rows.pop(k, None)
        if not last:
            q = q * scale
            qs = [row_splat(q, j) for j in range(8)]

            def update(v, c):
                t0 = c[0] * qs[0] + c[1] * qs[1]
                t1 = c[2] * qs[2] + c[3] * qs[3]
                t2 = c[4] * qs[4] + c[5] * qs[5]
                t3 = c[6] * qs[6] + c[7] * qs[7]
                return jnp.where(own, 0.0, v) - ((t0 + t1) + (t2 + t3))

            rows[k + 1] = update(following, ahead)
            cols = later
            for r in range(k + 2, n):
                v = take(r)
                rows[r] = update(v, [lane_splat(v, 8 * k + j) for j in range(8)])


ROWS_AT, COLS_AT = 8, 32
NT = NL + NR
ROWS = NR * W


def three_left(x):
    high, low = split(x)
    return jnp.concatenate([high, high, low], axis=1)


def three_right(x, axis):
    high, low = split(x)
    return jnp.concatenate([high, low, high], axis=axis)


def bdot(a, b):
    return lax.dot_general(a, b, (((1,), (0,)), ((), ())), preferred_element_type=F32)


def bdot_nt(a, b):
    return lax.dot_general(a, b, (((1,), (1,)), ((), ())), preferred_element_type=F32)


def prepare_points(r, c, v):
    same, jmask = eye_masks()
    lane = lax.broadcasted_iota(jnp.int32, (W, W), 1)
    square = v.square
    square[...] = jnp.zeros((W, W), F32)
    square[0:8, :] = v.padded[0:8, :]
    square[ROWS_AT:ROWS_AT + 16, :] = v.padded[pl.ds(NR * r, 16), :]
    square[COLS_AT:COLS_AT + 24, :] = v.padded[pl.ds(NC * c, 24), :]
    t = square[...].T
    for i in range(NL):
        for j in range(NL):
            a_row, b_row = square[i:i + 1, :], square[j:j + 1, :]
            part = tile(kval(a_row, b_row), a_row, b_row, t[:, i:i + 1], t[:, j:j + 1], jmask)
            if i == j:
                part = part + jnp.where(same, v.noise[i:i + 1, :], 0.0)
            v.work[W * i:W * i + W, W * j:W * j + W] = part
    colp = square[COLS_AT:COLS_AT + 24, :]
    coef = []
    total = []
    for m in range(NL):
        km = kval(colp, square[m:m + 1, :])
        v.table[m, :, :] = jnp.broadcast_to(km, (24, W))
        q = -km * (unit_row() + colp - square[m:m + 1, :])
        total.append(q)
        pieces = [q if n == m else jnp.zeros((24, W), F32) for n in range(NL)]
        coef.append(jnp.concatenate(pieces, axis=1))
    weights = jnp.concatenate([jnp.concatenate(total, axis=1)] + coef + [jnp.zeros((W - 24 * (NL + 1), LEAD), F32)], axis=0)
    v.f3[0:W, :] = three_right(weights, 1)
    tc = pltpu.roll(t, W - COLS_AT, 1)
    for i in range(NR):
        a_row = square[ROWS_AT + i:ROWS_AT + i + 1, :]
        a_col = t[:, ROWS_AT + i:ROWS_AT + i + 1]
        rows = slice(W * i, W * i + W)
        for l in range(NL):
            b_row = square[l:l + 1, :]
            part = tile(kval(a_row, b_row), a_row, b_row, a_col, t[:, l:l + 1], jmask)
            if l == i:
                part = part + jnp.where(same & (r == 0), v.noise[l:l + 1, :], 0.0)
            v.own[rows, W * l:W * l + W] = part
        rho = tc - a_col
        kk = jnp.exp(-0.5 * jnp.sum(rho * rho, axis=0, keepdims=True))
        v.kp[rows, :] = jnp.where((lane < NC) & ((r > 0) | (i >= NL)), kk * (unit_col() + rho), 0.0)
        alive = jnp.where(r == 0, 0.0, 1.0) if i < NL else 1.0
        v.table[NL + i, :, :] = jnp.broadcast_to(kval(colp, a_row) * alive, (24, W))
        v.h[rows, LEAD:LEAD + W] = jnp.where(jmask, -1.0, 0.0) + a_col * a_row


def factor(v, after):
    work, m_ref = v.work, v.m
    work[...] += dot_nt(v.lead[...], v.lead[...])
    for p in range(NL):
        lo, hi = W * p, W * p + W

        def write(k, x):
            m_ref[lo + 8 * k:lo + 8 * k + 8, lo:hi] = x

        invert_block(lambda k: work[lo + 8 * k:lo + 8 * k + 8, lo:hi], write)
        inv = m_ref[lo:hi, lo:hi]
        if p:
            m_ref[lo:hi, 0:lo] = dot(inv, work[lo:hi, 0:lo])
        if hi < LEAD:
            m_ref[lo:hi, hi:] = jnp.zeros((W, LEAD - hi), F32)
            u = dot(inv, work[lo:hi, hi:])
            work[hi:, hi:] -= dot_tn(u, u)
            e = dot_tn(u, m_ref[lo:hi, 0:hi])
            if p:
                work[hi:, 0:lo] -= e[:, 0:lo]
            work[hi:, lo:hi] = -e[:, lo:hi]
        after(p)


def prepare_rows(r, c, v):
    for s in range(NR // 2):
        rows = slice(2 * W * s, 2 * W * s + 2 * W)
        v.own[rows, :] += bdot_nt(three_left(v.basis[rows, :]), v.l3[...])
    g = bdot(three_left(v.m[...].T), three_right(v.m[...], 0))
    g3 = three_right(g, 0)
    for s in range(NR // 2):
        rows = slice(2 * W * s, 2 * W * s + 2 * W)
        hs = bdot(three_left(v.own[rows, :]), g3)
        b = v.basis[rows, :]
        if s < NL // 2:
            hs = jnp.where(r == 0, -v.m[rows, :], hs)
            b = jnp.where(r == 0, 0.0, b)
        for m in range(NL):
            v.h[rows, W * m:W * m + W] = jnp.where(lax.broadcasted_iota(jnp.int32, (2 * W, W), 1) > 0, hs[:, W * m:W * m + W], 0.0)
        eb = bdot_nt(three_left(hs), v.f3[...])
        v.lhs[rows, 0:3 * W] = three_left(b - eb[:, W:])
        v.lhs[rows, 3 * W:] = three_left(eb[:, 0:W] + v.kp[rows, :])

    @pl.when(c == 0)
    def _():
        m3 = three_left(v.m[...])
        for s in range(NR // 2):
            rows = slice(2 * W * s, 2 * W * s + 2 * W)
            x = bdot_nt(three_right(v.own[rows, :], 1), m3)
            rid = 2 * W * s + lax.broadcasted_iota(jnp.int32, (2 * W, LEAD), 0)
            cid = lax.broadcasted_iota(jnp.int32, (2 * W, LEAD), 1)
            v.panel[rows, :] = jnp.where((r == 0) & (rid < cid), 0.0, x)


def pad_points(v, raw):
    n = raw.shape[0]
    v.padded[0:n, :] = jnp.concatenate([jnp.zeros((n, 1), F32), raw[...]], axis=1)
    v.padded[n:, :] = jnp.zeros((v.padded.shape[0] - n, W), F32)


def lead_products(v):
    v.l3[...] = three_right(v.lead[...], 1)
    v.f3[W:2 * W, :] = three_right(v.lead[...].T, 1)


OUTS = (("square", (W, W), F32), ("table", (NT, 24, W), F32), ("h", (ROWS, LEAD + W), F32), ("lhs", (ROWS, 6 * W), BF),
        ("panel", (ROWS, LEAD), F32))
WORK = (("padded", (192, W), F32), ("lead", (LEAD, W), F32), ("noise", (8, W), F32), ("basis", (ROWS, W), F32),
        ("m", (LEAD, LEAD), F32), ("work", (LEAD, LEAD), F32), ("own", (ROWS, LEAD), F32), ("kp", (ROWS, W), F32),
        ("f3", (2 * W, 3 * LEAD), BF), ("l3", (LEAD, 3 * W), BF))


def lead_kernel(points_hbm, noise_hbm, basis_hbm, *refs):
    n = len(OUTS)
    v = SimpleNamespace(**dict(zip([o[0] for o in OUTS], refs[:n])))
    cols_ref = refs[n]
    refs = refs[n + 1:]
    for spec, ref in zip(WORK, refs):
        setattr(v, spec[0], ref)
    stage, raw, in_sem, *sems = refs[len(WORK):]
    moves = Moves(basis_hbm, v.lead, stage, cols_ref, sems)
    copies = [
        pltpu.make_async_copy(points_hbm, raw, in_sem.at[0]),
        pltpu.make_async_copy(noise_hbm.at[pl.ds(0, 8)], v.noise, in_sem.at[1]),
        pltpu.make_async_copy(basis_hbm, v.basis, in_sem.at[2]),
    ]
    for copy in copies:
        copy.start()
    moves.barrier()
    moves.start_spread()
    for copy in copies:
        copy.wait()
    pad_points(v, raw)
    prepare_points(moves.r, moves.c, v)
    moves.finish_spread()
    moves.start_z()
    lead_products(v)

    def after(p):
        if p < 2:
            for n in range(CHUNKS // 2):
                moves.forward(CHUNKS // 2 * p + n)

    factor(v, after)
    prepare_rows(moves.r, moves.c, v)
    moves.finish()


def prepare(points, noise, basis):
    vmem = pl.BlockSpec(memory_space=pltpu.VMEM)
    dma = pltpu.SemaphoreType.DMA
    return pl.pallas_call(
        lead_kernel,
        out_shape=tuple(jax.ShapeDtypeStruct(o[1], o[2]) for o in OUTS) + (jax.ShapeDtypeStruct((NC * W, W), F32),),
        in_specs=[pl.BlockSpec(memory_space=pl.ANY)] * 3,
        out_specs=(vmem,) * (len(OUTS) + 1),
        scratch_shapes=[pltpu.VMEM(o[1], o[2]) for o in WORK] + [
            pltpu.VMEM((BLOCK_HALF, W), F32),
            pltpu.VMEM(points.shape, F32),
            dma((3,)),
            dma((RG,)),
            dma((RG,)),
            dma((RG,)),
            dma((2,)),
            dma((1 + 2 * CHUNKS,)),
            dma((CHUNKS, 4)),
            dma((CHUNKS,)),
            dma((CHUNKS, 4)),
            dma((2, 2, CHUNKS)),
        ],
        compiler_params=pltpu.CompilerParams(collective_id=0, has_side_effects=True, vmem_limit_bytes=32 << 20),
    )(points, noise, basis)


def finish_kernel(pos, square, table, h, lhs, panel, cols_ref, noise_ref, out_ref, rhs):
    r, c = pos()
    step = pl.program_id(0)
    same, _ = eye_masks()
    is_panel = (c == 0) & (step < 2)

    @pl.when(is_panel)
    def _():
        out_ref[...] = panel[:, pl.ds(pl.multiple_of(256 * jnp.minimum(step, 1), 256), 256)]

    @pl.when(jnp.logical_not(is_panel))
    def _():
        b = cols_ref[pl.ds(pl.multiple_of(256 * step, 256), 256), :]
        rhs[0:3 * W, :] = three_right(b.T, 0)
        bases = []
        row_idx = lax.broadcasted_iota(jnp.int32, (W, W), 0)
        for s in range(2):
            j = 2 * step + s
            y = square[pl.ds(COLS_AT + j, 1), :]
            ycol = jnp.sum(jnp.where(same, y, 0.0), axis=1, keepdims=True)
            bases.append(jnp.broadcast_to(unit_col() + ycol, (W, W)))
            v = jnp.where(row_idx == j, unit_row() - y, 0.0)
            for m in range(NL):
                v = v + jnp.where(row_idx == 24 + 24 * m + j, square[m:m + 1, :], 0.0)
            rhs[3 * W:, W * s:W * s + W] = three_right(v, 0)

        def rows_block(s):
            rows = slice(256 * s, 256 * s + 256)
            acc = bdot(lhs[rows, :], rhs[...])
            for ii in range(2):
                i = 2 * s + ii
                at = slice(W * i, W * i + W)
                y_i = square[ROWS_AT + i:ROWS_AT + i + 1, :]
                his = [h[at, W * m:W * m + W] for m in range(NL + 1)]
                for jj in range(2):
                    ks = [table[m, pl.ds(2 * step + jj, 1), :] for m in range(NL)]
                    ks.append(table[NL + i, pl.ds(2 * step + jj, 1), :])
                    v = acc[W * ii:W * ii + W, W * jj:W * jj + W] + bases[jj] * (ks[NL] * y_i)
                    comb = (ks[0] * his[0] + ks[1] * his[1]) + (ks[2] * his[2] + ks[3] * his[3])
                    out_ref[at, W * jj:W * jj + W] = v - (comb + ks[4] * his[4])

        for s in range(5):
            rows_block(s)

        for s in range(2):
            i = NC * c + 2 * step + s - NR * r

            @pl.when((i >= 0) & (i < NR) & ((r > 0) | (i >= NL)))
            def _():
                at = pl.ds(pl.multiple_of(W * i, W), W)
                out_ref[at, W * s:W * s + W] += jnp.where(same, noise_ref[pl.ds(NR * r + i, 1), :], 0.0)


def finish_call(pos, prepared, noise):
    full = pl.BlockSpec(memory_space=pltpu.VMEM)
    return pl.pallas_call(
        lambda *refs: finish_kernel(pos, *refs),
        grid=(NC // 2,),
        out_shape=jax.ShapeDtypeStruct((ROWS, NC * W), F32),
        in_specs=[full] * 7,
        out_specs=pl.BlockSpec((ROWS, 2 * W), lambda s: (0, s)),
        scratch_shapes=[pltpu.VMEM((6 * W, 2 * W), BF)],
        compiler_params=pltpu.CompilerParams(vmem_limit_bytes=32 << 20),
    )(*prepared, noise)


def body(points, noise, basis):
    prepared = prepare(points, noise, basis)

    def pos():
        return lax.axis_index("rows"), lax.axis_index("cols")

    return finish_call(pos, prepared, noise)


def solution(mesh):
    placed = (P(), P(), P("rows", None))
    return jax.shard_map(body, mesh=mesh, in_specs=placed, out_specs=P("rows", "cols"), check_vma=False)
```

```python
from types import SimpleNamespace

import jax
import jax.numpy as jnp
from jax import lax
from jax.experimental import pallas as pl
from jax.experimental.pallas import tpu as pltpu
from jax.sharding import PartitionSpec as P

W = 128
LEAD = 512
NL = LEAD // W
NR = 10
NC = 20
RG = 16
HALF = LEAD // 2
PIECE = HALF // RG
BLOCK_HALF = NR * W // 2
CHUNKS = 4
CHUNK = BLOCK_HALF // CHUNKS
MESH = pl.DeviceIdType.MESH
HI = lax.Precision.HIGHEST
F32 = jnp.float32
BF = jnp.bfloat16


def dot(a, b):
    return lax.dot_general(a, b, (((1,), (0,)), ((), ())), precision=HI, preferred_element_type=F32)


def dot_nt(a, b):
    return lax.dot_general(a, b, (((1,), (1,)), ((), ())), precision=HI, preferred_element_type=F32)


def dot_tn(a, b):
    return lax.dot_general(a, b, (((0,), (0,)), ((), ())), precision=HI, preferred_element_type=F32)


def split(x):
    high = x.astype(BF)
    return high, (x - high.astype(F32)).astype(BF)


class Moves:
    def __init__(self, basis, lead, stage, cols, sems):
        self.basis, self.lead, self.stage, self.cols = basis, lead, stage, cols
        (self.first_sem, self.second_sem, self.lead_recv, self.half_sem, self.local_sem,
         self.a_send, self.a_recv, self.b_send, self.b_recv) = sems
        self.r = lax.axis_index("rows")
        self.c = lax.axis_index("cols")
        self.z, self.x = self.r // 4, self.r % 4
        self.y, self.k = self.c // 2, self.c % 2
        self.home = self.x // 2

    def barrier(self):
        sem = pltpu.get_barrier_semaphore()
        for off in range(1, RG):
            pl.semaphore_signal(sem, inc=1, device_id=((self.r + off) % RG, self.c), device_id_type=MESH)
        for x in range(4):
            pl.semaphore_signal(sem, inc=1, device_id=(4 * self.z + x, 2 * self.y + 1 - self.k), device_id_type=MESH)
        pl.semaphore_wait(sem, RG + 3)

    def piece(self, source, q, send_sem, target):
        rows = pl.ds(pl.multiple_of(HALF * self.k + PIECE * q, PIECE), PIECE)
        return pltpu.make_async_remote_copy(
            src_ref=source.at[rows], dst_ref=self.lead.at[rows], send_sem=send_sem, recv_sem=self.lead_recv.at[q],
            device_id=(target, self.c), device_id_type=MESH)

    def exchange(self, core):
        rows = pl.ds(pl.multiple_of(HALF * core, HALF), HALF)
        return pltpu.make_async_remote_copy(
            src_ref=self.lead.at[rows], dst_ref=self.lead.at[rows], send_sem=self.half_sem.at[0], recv_sem=self.half_sem.at[1],
            device_id=(self.r, 2 * self.y + 1 - self.k), device_id_type=MESH)

    def start_spread(self):
        @pl.when(self.r == 0)
        def _():
            for t in range(1, RG):
                self.piece(self.basis, t, self.first_sem.at[t], t).start()
            for t in range(1, RG):
                self.piece(self.basis, 0, self.second_sem.at[t], t).start()
            pltpu.make_async_copy(self.basis.at[pl.ds(0, LEAD)], self.lead, self.local_sem.at[0]).start()

        @pl.when(self.r != 0)
        def _():
            self.piece(self.lead, self.r, self.first_sem.at[0], 0).wait_recv()
            for off in range(1, RG):
                @pl.when(self.r + off != RG)
                def _():
                    self.piece(self.lead, self.r, self.second_sem.at[off], (self.r + off) % RG).start()

    def finish_spread(self):
        @pl.when(self.r == 0)
        def _():
            pltpu.make_async_copy(self.basis.at[pl.ds(0, LEAD)], self.lead, self.local_sem.at[0]).wait()
            for t in range(1, RG):
                self.piece(self.basis, t, self.first_sem.at[t], t).wait_send()
                self.piece(self.basis, 0, self.second_sem.at[t], t).wait_send()

        @pl.when(self.r != 0)
        def _():
            for off in range(1, RG):
                self.piece(self.lead, (self.r + off) % RG, self.first_sem.at[0], 0).wait_recv()
            self.exchange(self.k).start()
            self.exchange(1 - self.k).wait_recv()
            self.exchange(self.k).wait_send()
            for off in range(1, RG):
                @pl.when(self.r + off != RG)
                def _():
                    self.piece(self.lead, self.r, self.second_sem.at[off], (self.r + off) % RG).wait_send()

    def own_rows(self, n):
        return pl.ds(pl.multiple_of(BLOCK_HALF * self.k + CHUNK * n, CHUNK), CHUNK)

    def along_z(self, n, dz):
        return pltpu.make_async_remote_copy(
            src_ref=self.basis.at[self.own_rows(n)], dst_ref=self.stage.at[pl.ds(CHUNK * n, CHUNK)],
            send_sem=self.a_send.at[n, dz], recv_sem=self.a_recv.at[n],
            device_id=(4 * ((self.z + dz) % 4) + self.x, self.c), device_id_type=MESH)

    def keep(self, n):
        return pltpu.make_async_copy(self.basis.at[self.own_rows(n)], self.stage.at[pl.ds(CHUNK * n, CHUNK)], self.local_sem.at[1 + n])

    def start_z(self):
        @pl.when(self.z == self.y)
        def _():
            for n in range(CHUNKS):
                for dz in (1, 3, 2):
                    self.along_z(n, dz).start()
                self.keep(n).start()

    def place(self, block, half, n):
        return pl.ds(pl.multiple_of(2 * BLOCK_HALF * block + BLOCK_HALF * half + CHUNK * n, CHUNK), CHUNK)

    def along_x(self, n, dx):
        return pltpu.make_async_remote_copy(
            src_ref=self.stage.at[pl.ds(CHUNK * n, CHUNK)], dst_ref=self.cols.at[self.place(self.x % 2, self.k, n)],
            send_sem=self.b_send.at[n, dx], recv_sem=self.b_recv.at[self.x % 2, self.k, n],
            device_id=(4 * self.z + (self.x + dx) % 4, 2 * self.y + self.home), device_id_type=MESH)

    def settle(self, n):
        return pltpu.make_async_copy(self.stage.at[pl.ds(CHUNK * n, CHUNK)], self.cols.at[self.place(self.x % 2, self.k, n)], self.local_sem.at[1 + CHUNKS + n])

    def forward(self, n):
        @pl.when(self.z == self.y)
        def _():
            self.keep(n).wait()

        @pl.when(self.z != self.y)
        def _():
            self.along_z(n, 1).wait_recv()

        for dx in (1, 3, 2):
            self.along_x(n, dx).start()

        @pl.when(self.home == self.k)
        def _():
            self.settle(n).start()

        @pl.when(self.home != self.k)
        def _():
            self.along_x(n, 0).start()

    def finish(self):
        for n in range(CHUNKS):
            for block in range(2):
                for half in range(2):
                    mine = (self.home == self.k) & (self.x % 2 == block) & (self.k == half)

                    @pl.when(jnp.logical_not(mine))
                    def _():
                        rows = self.place(block, half, n)
                        pltpu.make_async_remote_copy(
                            src_ref=self.cols.at[rows], dst_ref=self.cols.at[rows], send_sem=self.b_send.at[n, 0],
                            recv_sem=self.b_recv.at[block, half, n],
                            device_id=(self.r, 2 * self.y + 1 - self.k), device_id_type=MESH).wait_recv()
        for n in range(CHUNKS):
            for dx in (1, 3, 2):
                self.along_x(n, dx).wait_send()

            @pl.when(self.home == self.k)
            def _():
                self.settle(n).wait()

            @pl.when(self.home != self.k)
            def _():
                self.along_x(n, 0).wait_send()

            @pl.when(self.z == self.y)
            def _():
                for dz in (1, 3, 2):
                    self.along_z(n, dz).wait_send()


def eye_masks():
    row = lax.broadcasted_iota(jnp.int32, (W, W), 0)
    col = lax.broadcasted_iota(jnp.int32, (W, W), 1)
    same = row == col
    return same, same & (col > 0)


def unit_row():
    return (lax.broadcasted_iota(jnp.int32, (1, W), 1) == 0).astype(F32)


def unit_col():
    return (lax.broadcasted_iota(jnp.int32, (W, 1), 0) == 0).astype(F32)


def kval(a_row, b_row):
    rho = a_row - b_row
    return jnp.exp(-0.5 * jnp.sum(rho * rho, axis=1, keepdims=True))


def tile(k, a_row, b_row, a_col, b_col, jmask):
    p = k * (unit_col() + b_col - a_col)
    q = unit_row() + a_row - b_row
    return jnp.where(jmask, k, 0.0) + p * q


def lane_splat(v, j):
    return jnp.broadcast_to(v[:, j:j + 1], (8, W))


def row_splat(v, j):
    return jnp.broadcast_to(v[j:j + 1, :], (8, W))


def invert_block(read, write):
    n = W // 8
    lane = lax.broadcasted_iota(jnp.int32, (8, W), 1)
    sub = lax.broadcasted_iota(jnp.int32, (8, W), 0)
    rows = {}

    def take(r):
        return rows[r] if r in rows else read(r)

    cols = [lane_splat(take(0), j) for j in range(8)]
    for k in range(n):
        own = (lane >= 8 * k) & (lane < 8 * k + 8)
        last = k + 1 == n
        if not last:
            following = take(k + 1)
            ahead = [lane_splat(following, 8 * k + j) for j in range(8)]
            below = list(ahead)
            later = [lane_splat(following, 8 * k + 8 + j) for j in range(8)]
        q = jnp.where(own, (lane - 8 * k == sub).astype(F32), take(k))
        w = scale = None
        for j in range(8):
            d = row_splat(cols[j], j)
            inv = 1.0 / d
            row_j = row_splat(q, j)
            others = jnp.where(sub == j, 0.0, cols[j])
            pivots = {j2: row_splat(cols[j2], j) for j2 in range(j + 1, 8)}
            for j2 in range(j + 1, 8):
                cols[j2] = cols[j2] - inv * (others * pivots[j2])
            q = q - inv * (others * row_j)
            w_j = row_j * lax.rsqrt(d)
            w = w_j if w is None else jnp.where(sub == j, w_j, w)
            scale = inv if scale is None else jnp.where(sub == j, inv, scale)
            if not last:
                m = below[j] * inv
                for j2 in range(j + 1, 8):
                    below[j2] = below[j2] - m * pivots[j2]
                for j2 in range(8):
                    later[j2] = later[j2] - m * row_splat(below[j], j2)
        write(k, jnp.where(lane <= 8 * k + sub, w, 0.0))
        rows.pop(k, None)
        if not last:
            q = q * scale
            qs = [row_splat(q, j) for j in range(8)]

            def update(v, c):
                t0 = c[0] * qs[0] + c[1] * qs[1]
                t1 = c[2] * qs[2] + c[3] * qs[3]
                t2 = c[4] * qs[4] + c[5] * qs[5]
                t3 = c[6] * qs[6] + c[7] * qs[7]
                return jnp.where(own, 0.0, v) - ((t0 + t1) + (t2 + t3))

            rows[k + 1] = update(following, ahead)
            cols = later
            for r in range(k + 2, n):
                v = take(r)
                rows[r] = update(v, [lane_splat(v, 8 * k + j) for j in range(8)])


ROWS_AT, COLS_AT = 8, 32
NT = NL + NR
ROWS = NR * W


def three_left(x):
    high, low = split(x)
    return jnp.concatenate([high, high, low], axis=1)


def three_right(x, axis):
    high, low = split(x)
    return jnp.concatenate([high, low, high], axis=axis)


def bdot(a, b):
    return lax.dot_general(a, b, (((1,), (0,)), ((), ())), preferred_element_type=F32)


def bdot_nt(a, b):
    return lax.dot_general(a, b, (((1,), (1,)), ((), ())), preferred_element_type=F32)


def prepare_points(r, c, v):
    same, jmask = eye_masks()
    lane = lax.broadcasted_iota(jnp.int32, (W, W), 1)
    square = v.square
    square[...] = jnp.zeros((W, W), F32)
    square[0:8, :] = v.padded[0:8, :]
    square[ROWS_AT:ROWS_AT + 16, :] = v.padded[pl.ds(NR * r, 16), :]
    square[COLS_AT:COLS_AT + 24, :] = v.padded[pl.ds(NC * c, 24), :]
    t = square[...].T
    for i in range(NL):
        for j in range(NL):
            a_row, b_row = square[i:i + 1, :], square[j:j + 1, :]
            part = tile(kval(a_row, b_row), a_row, b_row, t[:, i:i + 1], t[:, j:j + 1], jmask)
            if i == j:
                part = part + jnp.where(same, v.noise[i:i + 1, :], 0.0)
            v.work[W * i:W * i + W, W * j:W * j + W] = part
    colp = square[COLS_AT:COLS_AT + 24, :]
    coef = []
    total = []
    for m in range(NL):
        km = kval(colp, square[m:m + 1, :])
        v.table[m, :, :] = jnp.broadcast_to(km, (24, W))
        q = -km * (unit_row() + colp - square[m:m + 1, :])
        total.append(q)
        pieces = [q if n == m else jnp.zeros((24, W), F32) for n in range(NL)]
        coef.append(jnp.concatenate(pieces, axis=1))
    weights = jnp.concatenate([jnp.concatenate(total, axis=1)] + coef + [jnp.zeros((W - 24 * (NL + 1), LEAD), F32)], axis=0)
    v.f3[0:W, :] = three_right(weights, 1)
    tc = pltpu.roll(t, W - COLS_AT, 1)
    for i in range(NR):
        a_row = square[ROWS_AT + i:ROWS_AT + i + 1, :]
        a_col = t[:, ROWS_AT + i:ROWS_AT + i + 1]
        rows = slice(W * i, W * i + W)
        for l in range(NL):
            b_row = square[l:l + 1, :]
            part = tile(kval(a_row, b_row), a_row, b_row, a_col, t[:, l:l + 1], jmask)
            if l == i:
                part = part + jnp.where(same & (r == 0), v.noise[l:l + 1, :], 0.0)
            v.own[rows, W * l:W * l + W] = part
        rho = tc - a_col
        kk = jnp.exp(-0.5 * jnp.sum(rho * rho, axis=0, keepdims=True))
        v.kp[rows, :] = jnp.where((lane < NC) & ((r > 0) | (i >= NL)), kk * (unit_col() + rho), 0.0)
        alive = jnp.where(r == 0, 0.0, 1.0) if i < NL else 1.0
        v.table[NL + i, :, :] = jnp.broadcast_to(kval(colp, a_row) * alive, (24, W))
        v.h[rows, LEAD:LEAD + W] = jnp.where(jmask, -1.0, 0.0) + a_col * a_row


def factor(v, after):
    work, m_ref = v.work, v.m
    work[...] += dot_nt(v.lead[...], v.lead[...])
    for p in range(NL):
        lo, hi = W * p, W * p + W

        def write(k, x):
            m_ref[lo + 8 * k:lo + 8 * k + 8, lo:hi] = x

        invert_block(lambda k: work[lo + 8 * k:lo + 8 * k + 8, lo:hi], write)
        inv = m_ref[lo:hi, lo:hi]
        if p:
            m_ref[lo:hi, 0:lo] = dot(inv, work[lo:hi, 0:lo])
        if hi < LEAD:
            m_ref[lo:hi, hi:] = jnp.zeros((W, LEAD - hi), F32)
            u = dot(inv, work[lo:hi, hi:])
            work[hi:, hi:] -= dot_tn(u, u)
            e = dot_tn(u, m_ref[lo:hi, 0:hi])
            if p:
                work[hi:, 0:lo] -= e[:, 0:lo]
            work[hi:, lo:hi] = -e[:, lo:hi]
        after(p)
        part = m_ref[lo:hi, :]
        g = bdot(three_left(part.T), three_right(part, 0))
        v.g[...] = g if p == 0 else v.g[...] + g
        for s in ((0, 1), (2, 3), (4,), ())[p]:
            rows = slice(2 * W * s, 2 * W * s + 2 * W)
            v.own[rows, :] += bdot_nt(three_left(v.basis[rows, :]), v.l3[...])


def prepare_rows(r, c, v):
    g3 = three_right(v.g[...], 0)
    for s in range(NR // 2):
        rows = slice(2 * W * s, 2 * W * s + 2 * W)
        hs = bdot(three_left(v.own[rows, :]), g3)
        b = v.basis[rows, :]
        if s < NL // 2:
            hs = jnp.where(r == 0, -v.m[rows, :], hs)
            b = jnp.where(r == 0, 0.0, b)
        for m in range(NL):
            v.h[rows, W * m:W * m + W] = jnp.where(lax.broadcasted_iota(jnp.int32, (2 * W, W), 1) > 0, hs[:, W * m:W * m + W], 0.0)
        eb = bdot_nt(three_left(hs), v.f3[...])
        v.lhs[rows, 0:3 * W] = three_left(b - eb[:, W:])
        v.lhs[rows, 3 * W:] = three_left(eb[:, 0:W] + v.kp[rows, :])

    @pl.when(c == 0)
    def _():
        m3 = three_left(v.m[...])
        for s in range(NR // 2):
            rows = slice(2 * W * s, 2 * W * s + 2 * W)
            x = bdot_nt(three_right(v.own[rows, :], 1), m3)
            rid = 2 * W * s + lax.broadcasted_iota(jnp.int32, (2 * W, LEAD), 0)
            cid = lax.broadcasted_iota(jnp.int32, (2 * W, LEAD), 1)
            v.panel[rows, :] = jnp.where((r == 0) & (rid < cid), 0.0, x)


def pad_points(v, raw):
    n = raw.shape[0]
    v.padded[0:n, :] = jnp.concatenate([jnp.zeros((n, 1), F32), raw[...]], axis=1)
    v.padded[n:, :] = jnp.zeros((v.padded.shape[0] - n, W), F32)


def lead_products(v):
    v.l3[...] = three_right(v.lead[...], 1)
    v.f3[W:2 * W, :] = three_right(v.lead[...].T, 1)


OUTS = (("square", (W, W), F32), ("table", (NT, 24, W), F32), ("h", (ROWS, LEAD + W), F32), ("lhs", (ROWS, 6 * W), BF),
        ("panel", (ROWS, LEAD), F32), ("noise", (NR * RG, W), F32))
WORK = (("padded", (192, W), F32), ("lead", (LEAD, W), F32), ("basis", (ROWS, W), F32),
        ("m", (LEAD, LEAD), F32), ("g", (LEAD, LEAD), F32), ("work", (LEAD, LEAD), F32), ("own", (ROWS, LEAD), F32), ("kp", (ROWS, W), F32),
        ("f3", (2 * W, 3 * LEAD), BF), ("l3", (LEAD, 3 * W), BF))


def lead_kernel(points_hbm, noise_hbm, basis_hbm, *refs):
    n = len(OUTS)
    v = SimpleNamespace(**dict(zip([o[0] for o in OUTS], refs[:n])))
    cols_ref = refs[n]
    refs = refs[n + 1:]
    for spec, ref in zip(WORK, refs):
        setattr(v, spec[0], ref)
    stage, raw, in_sem, *sems = refs[len(WORK):]
    moves = Moves(basis_hbm, v.lead, stage, cols_ref, sems)
    copies = [
        pltpu.make_async_copy(points_hbm, raw, in_sem.at[0]),
        pltpu.make_async_copy(noise_hbm, v.noise, in_sem.at[1]),
        pltpu.make_async_copy(basis_hbm, v.basis, in_sem.at[2]),
    ]
    for copy in copies:
        copy.start()
    moves.barrier()
    moves.start_spread()
    for copy in copies:
        copy.wait()
    pad_points(v, raw)
    prepare_points(moves.r, moves.c, v)
    moves.finish_spread()
    moves.start_z()
    lead_products(v)

    def after(p):
        moves.forward(p)

    factor(v, after)
    prepare_rows(moves.r, moves.c, v)
    moves.finish()


def prepare(points, noise, basis):
    vmem = pl.BlockSpec(memory_space=pltpu.VMEM)
    dma = pltpu.SemaphoreType.DMA
    return pl.pallas_call(
        lead_kernel,
        out_shape=tuple(jax.ShapeDtypeStruct(o[1], o[2]) for o in OUTS) + (jax.ShapeDtypeStruct((NC * W, W), F32),),
        in_specs=[pl.BlockSpec(memory_space=pl.ANY)] * 3,
        out_specs=(vmem,) * (len(OUTS) + 1),
        scratch_shapes=[pltpu.VMEM(o[1], o[2]) for o in WORK] + [
            pltpu.VMEM((BLOCK_HALF, W), F32),
            pltpu.VMEM(points.shape, F32),
            dma((3,)),
            dma((RG,)),
            dma((RG,)),
            dma((RG,)),
            dma((2,)),
            dma((1 + 2 * CHUNKS,)),
            dma((CHUNKS, 4)),
            dma((CHUNKS,)),
            dma((CHUNKS, 4)),
            dma((2, 2, CHUNKS)),
        ],
        compiler_params=pltpu.CompilerParams(collective_id=0, has_side_effects=True, vmem_limit_bytes=32 << 20),
    )(*[pltpu.with_memory_space_constraint(a, pltpu.HBM) for a in (points, noise, basis)])


def finish_kernel(pos, square, table, h, lhs, panel, noise_ref, cols_ref, out_ref, rhs):
    r, c = pos()
    step = pl.program_id(0)
    same, _ = eye_masks()
    is_panel = (c == 0) & (step < 2)

    @pl.when(is_panel)
    def _():
        out_ref[...] = panel[:, pl.ds(pl.multiple_of(256 * jnp.minimum(step, 1), 256), 256)]

    @pl.when(jnp.logical_not(is_panel))
    def _():
        b = cols_ref[pl.ds(pl.multiple_of(256 * step, 256), 256), :]
        rhs[0:3 * W, :] = three_right(b.T, 0)
        bases = []
        row_idx = lax.broadcasted_iota(jnp.int32, (W, W), 0)
        for s in range(2):
            j = 2 * step + s
            y = square[pl.ds(COLS_AT + j, 1), :]
            ycol = jnp.sum(jnp.where(same, y, 0.0), axis=1, keepdims=True)
            bases.append(jnp.broadcast_to(unit_col() + ycol, (W, W)))
            v = jnp.where(row_idx == j, unit_row() - y, 0.0)
            for m in range(NL):
                v = v + jnp.where(row_idx == 24 + 24 * m + j, square[m:m + 1, :], 0.0)
            rhs[3 * W:, W * s:W * s + W] = three_right(v, 0)

        def rows_block(s):
            rows = slice(256 * s, 256 * s + 256)
            acc = bdot(lhs[rows, :], rhs[...])
            for ii in range(2):
                i = 2 * s + ii
                at = slice(W * i, W * i + W)
                y_i = square[ROWS_AT + i:ROWS_AT + i + 1, :]
                his = [h[at, W * m:W * m + W] for m in range(NL + 1)]
                for jj in range(2):
                    ks = [table[m, pl.ds(2 * step + jj, 1), :] for m in range(NL)]
                    ks.append(table[NL + i, pl.ds(2 * step + jj, 1), :])
                    v = acc[W * ii:W * ii + W, W * jj:W * jj + W] + bases[jj] * (ks[NL] * y_i)
                    comb = (ks[0] * his[0] + ks[1] * his[1]) + (ks[2] * his[2] + ks[3] * his[3])
                    out_ref[at, W * jj:W * jj + W] = v - (comb + ks[4] * his[4])

        for s in range(5):
            rows_block(s)

        for s in range(2):
            i = NC * c + 2 * step + s - NR * r

            @pl.when((i >= 0) & (i < NR) & ((r > 0) | (i >= NL)))
            def _():
                at = pl.ds(pl.multiple_of(W * i, W), W)
                out_ref[at, W * s:W * s + W] += jnp.where(same, noise_ref[pl.ds(NR * r + i, 1), :], 0.0)


def finish_call(pos, prepared):
    full = pl.BlockSpec(memory_space=pltpu.VMEM)
    return pl.pallas_call(
        lambda *refs: finish_kernel(pos, *refs),
        grid=(NC // 2,),
        out_shape=jax.ShapeDtypeStruct((ROWS, NC * W), F32),
        in_specs=[full] * 7,
        out_specs=pl.BlockSpec((ROWS, 2 * W), lambda s: (0, s)),
        scratch_shapes=[pltpu.VMEM((6 * W, 2 * W), BF)],
        compiler_params=pltpu.CompilerParams(vmem_limit_bytes=32 << 20),
    )(*prepared)


def body(points, noise, basis):
    prepared = prepare(points, noise, basis)

    def pos():
        return lax.axis_index("rows"), lax.axis_index("cols")

    return finish_call(pos, prepared)


def solution(mesh):
    placed = (P(), P(), P("rows", None))
    return jax.shard_map(body, mesh=mesh, in_specs=placed, out_specs=P("rows", "cols"), check_vma=False)
```

```python
from types import SimpleNamespace

import jax
import jax.numpy as jnp
from jax import lax
from jax.experimental import pallas as pl
from jax.experimental.pallas import tpu as pltpu
from jax.sharding import PartitionSpec as P

W = 128
LEAD = 512
NL = LEAD // W
NR = 10
NC = 20
RG = 16
HALF = LEAD // 2
PIECE = HALF // RG
BLOCK_HALF = NR * W // 2
CHUNKS = 4
CHUNK = BLOCK_HALF // CHUNKS
MESH = pl.DeviceIdType.MESH
HI = lax.Precision.HIGHEST
F32 = jnp.float32
BF = jnp.bfloat16


def dot(a, b):
    return lax.dot_general(a, b, (((1,), (0,)), ((), ())), precision=HI, preferred_element_type=F32)


def dot_nt(a, b):
    return lax.dot_general(a, b, (((1,), (1,)), ((), ())), precision=HI, preferred_element_type=F32)


def dot_tn(a, b):
    return lax.dot_general(a, b, (((0,), (0,)), ((), ())), precision=HI, preferred_element_type=F32)


def split(x):
    high = x.astype(BF)
    return high, (x - high.astype(F32)).astype(BF)


class Moves:
    def __init__(self, basis, lead, stage, cols, sems):
        self.basis, self.lead, self.stage, self.cols = basis, lead, stage, cols
        (self.first_sem, self.second_sem, self.lead_recv, self.half_sem, self.local_sem,
         self.a_send, self.a_recv, self.b_send, self.b_recv) = sems
        self.r = lax.axis_index("rows")
        self.c = lax.axis_index("cols")
        self.z, self.x = self.r // 4, self.r % 4
        self.y, self.k = self.c // 2, self.c % 2
        self.home = self.x // 2

    def barrier(self):
        sem = pltpu.get_barrier_semaphore()
        for off in range(1, RG):
            pl.semaphore_signal(sem, inc=1, device_id=((self.r + off) % RG, self.c), device_id_type=MESH)
        for x in range(4):
            pl.semaphore_signal(sem, inc=1, device_id=(4 * self.z + x, 2 * self.y + 1 - self.k), device_id_type=MESH)
        pl.semaphore_wait(sem, RG + 3)

    def piece(self, source, q, send_sem, target):
        rows = pl.ds(pl.multiple_of(HALF * self.k + PIECE * q, PIECE), PIECE)
        return pltpu.make_async_remote_copy(
            src_ref=source.at[rows], dst_ref=self.lead.at[rows], send_sem=send_sem, recv_sem=self.lead_recv.at[q],
            device_id=(target, self.c), device_id_type=MESH)

    def exchange(self, core):
        rows = pl.ds(pl.multiple_of(HALF * core, HALF), HALF)
        return pltpu.make_async_remote_copy(
            src_ref=self.lead.at[rows], dst_ref=self.lead.at[rows], send_sem=self.half_sem.at[0], recv_sem=self.half_sem.at[1],
            device_id=(self.r, 2 * self.y + 1 - self.k), device_id_type=MESH)

    def start_spread(self):
        @pl.when(self.r == 0)
        def _():
            for t in range(1, RG):
                self.piece(self.basis, t, self.first_sem.at[t], t).start()
            for t in range(1, RG):
                self.piece(self.basis, 0, self.second_sem.at[t], t).start()
            pltpu.make_async_copy(self.basis.at[pl.ds(0, LEAD)], self.lead, self.local_sem.at[0]).start()

        @pl.when(self.r != 0)
        def _():
            self.piece(self.lead, self.r, self.first_sem.at[0], 0).wait_recv()
            for off in range(1, RG):
                @pl.when(self.r + off != RG)
                def _():
                    self.piece(self.lead, self.r, self.second_sem.at[off], (self.r + off) % RG).start()

    def finish_spread(self):
        @pl.when(self.r == 0)
        def _():
            pltpu.make_async_copy(self.basis.at[pl.ds(0, LEAD)], self.lead, self.local_sem.at[0]).wait()
            for t in range(1, RG):
                self.piece(self.basis, t, self.first_sem.at[t], t).wait_send()
                self.piece(self.basis, 0, self.second_sem.at[t], t).wait_send()

        @pl.when(self.r != 0)
        def _():
            for off in range(1, RG):
                self.piece(self.lead, (self.r + off) % RG, self.first_sem.at[0], 0).wait_recv()
            self.exchange(self.k).start()
            self.exchange(1 - self.k).wait_recv()
            self.exchange(self.k).wait_send()
            for off in range(1, RG):
                @pl.when(self.r + off != RG)
                def _():
                    self.piece(self.lead, self.r, self.second_sem.at[off], (self.r + off) % RG).wait_send()

    def own_rows(self, n):
        return pl.ds(pl.multiple_of(BLOCK_HALF * self.k + CHUNK * n, CHUNK), CHUNK)

    def along_z(self, n, dz):
        return pltpu.make_async_remote_copy(
            src_ref=self.basis.at[self.own_rows(n)], dst_ref=self.stage.at[pl.ds(CHUNK * n, CHUNK)],
            send_sem=self.a_send.at[n, dz], recv_sem=self.a_recv.at[n],
            device_id=(4 * ((self.z + dz) % 4) + self.x, self.c), device_id_type=MESH)

    def keep(self, n):
        return pltpu.make_async_copy(self.basis.at[self.own_rows(n)], self.stage.at[pl.ds(CHUNK * n, CHUNK)], self.local_sem.at[1 + n])

    def start_z(self):
        @pl.when(self.z == self.y)
        def _():
            for n in range(CHUNKS):
                for dz in (1, 3, 2):
                    self.along_z(n, dz).start()
                self.keep(n).start()

    def place(self, block, half, n):
        return pl.ds(pl.multiple_of(2 * BLOCK_HALF * block + BLOCK_HALF * half + CHUNK * n, CHUNK), CHUNK)

    def along_x(self, n, dx):
        return pltpu.make_async_remote_copy(
            src_ref=self.stage.at[pl.ds(CHUNK * n, CHUNK)], dst_ref=self.cols.at[self.place(self.x % 2, self.k, n)],
            send_sem=self.b_send.at[n, dx], recv_sem=self.b_recv.at[self.x % 2, self.k, n],
            device_id=(4 * self.z + (self.x + dx) % 4, 2 * self.y + self.home), device_id_type=MESH)

    def settle(self, n):
        return pltpu.make_async_copy(self.stage.at[pl.ds(CHUNK * n, CHUNK)], self.cols.at[self.place(self.x % 2, self.k, n)], self.local_sem.at[1 + CHUNKS + n])

    def forward(self, n):
        @pl.when(self.z == self.y)
        def _():
            self.keep(n).wait()

        @pl.when(self.z != self.y)
        def _():
            self.along_z(n, 1).wait_recv()

        for dx in (1, 3, 2):
            self.along_x(n, dx).start()

        @pl.when(self.home == self.k)
        def _():
            self.settle(n).start()

        @pl.when(self.home != self.k)
        def _():
            self.along_x(n, 0).start()

    def finish(self):
        for n in range(CHUNKS):
            for block in range(2):
                for half in range(2):
                    mine = (self.home == self.k) & (self.x % 2 == block) & (self.k == half)

                    @pl.when(jnp.logical_not(mine))
                    def _():
                        rows = self.place(block, half, n)
                        pltpu.make_async_remote_copy(
                            src_ref=self.cols.at[rows], dst_ref=self.cols.at[rows], send_sem=self.b_send.at[n, 0],
                            recv_sem=self.b_recv.at[block, half, n],
                            device_id=(self.r, 2 * self.y + 1 - self.k), device_id_type=MESH).wait_recv()
        for n in range(CHUNKS):
            for dx in (1, 3, 2):
                self.along_x(n, dx).wait_send()

            @pl.when(self.home == self.k)
            def _():
                self.settle(n).wait()

            @pl.when(self.home != self.k)
            def _():
                self.along_x(n, 0).wait_send()

            @pl.when(self.z == self.y)
            def _():
                for dz in (1, 3, 2):
                    self.along_z(n, dz).wait_send()


def eye_masks():
    row = lax.broadcasted_iota(jnp.int32, (W, W), 0)
    col = lax.broadcasted_iota(jnp.int32, (W, W), 1)
    same = row == col
    return same, same & (col > 0)


def unit_row():
    return (lax.broadcasted_iota(jnp.int32, (1, W), 1) == 0).astype(F32)


def unit_col():
    return (lax.broadcasted_iota(jnp.int32, (W, 1), 0) == 0).astype(F32)


def kval(a_row, b_row):
    rho = a_row - b_row
    return jnp.exp(-0.5 * jnp.sum(rho * rho, axis=1, keepdims=True))


def tile(k, a_row, b_row, a_col, b_col, jmask):
    p = k * (unit_col() + b_col - a_col)
    q = unit_row() + a_row - b_row
    return jnp.where(jmask, k, 0.0) + p * q


def lane_splat(v, j):
    return jnp.broadcast_to(v[:, j:j + 1], (8, W))


def row_splat(v, j):
    return jnp.broadcast_to(v[j:j + 1, :], (8, W))


def invert_block(read, write):
    n = W // 8
    lane = lax.broadcasted_iota(jnp.int32, (8, W), 1)
    sub = lax.broadcasted_iota(jnp.int32, (8, W), 0)
    rows = {}

    def take(r):
        return rows[r] if r in rows else read(r)

    cols = [lane_splat(take(0), j) for j in range(8)]
    for k in range(n):
        own = (lane >= 8 * k) & (lane < 8 * k + 8)
        last = k + 1 == n
        if not last:
            following = take(k + 1)
            ahead = [lane_splat(following, 8 * k + j) for j in range(8)]
            below = list(ahead)
            later = [lane_splat(following, 8 * k + 8 + j) for j in range(8)]
        q = jnp.where(own, (lane - 8 * k == sub).astype(F32), take(k))
        w = scale = None
        for j in range(8):
            d = row_splat(cols[j], j)
            inv = 1.0 / d
            row_j = row_splat(q, j)
            others = jnp.where(sub == j, 0.0, cols[j])
            pivots = {j2: row_splat(cols[j2], j) for j2 in range(j + 1, 8)}
            for j2 in range(j + 1, 8):
                cols[j2] = cols[j2] - inv * (others * pivots[j2])
            q = q - inv * (others * row_j)
            w_j = row_j * lax.rsqrt(d)
            w = w_j if w is None else jnp.where(sub == j, w_j, w)
            scale = inv if scale is None else jnp.where(sub == j, inv, scale)
            if not last:
                m = below[j] * inv
                for j2 in range(j + 1, 8):
                    below[j2] = below[j2] - m * pivots[j2]
                for j2 in range(8):
                    later[j2] = later[j2] - m * row_splat(below[j], j2)
        write(k, jnp.where(lane <= 8 * k + sub, w, 0.0))
        rows.pop(k, None)
        if not last:
            q = q * scale
            qs = [row_splat(q, j) for j in range(8)]

            def update(v, c):
                t0 = c[0] * qs[0] + c[1] * qs[1]
                t1 = c[2] * qs[2] + c[3] * qs[3]
                t2 = c[4] * qs[4] + c[5] * qs[5]
                t3 = c[6] * qs[6] + c[7] * qs[7]
                return jnp.where(own, 0.0, v) - ((t0 + t1) + (t2 + t3))

            rows[k + 1] = update(following, ahead)
            cols = later
            for r in range(k + 2, n):
                v = take(r)
                rows[r] = update(v, [lane_splat(v, 8 * k + j) for j in range(8)])


ROWS_AT, COLS_AT = 8, 32
NT = NL + NR
ROWS = NR * W


def three_left(x):
    high, low = split(x)
    return jnp.concatenate([high, high, low], axis=1)


def three_right(x, axis):
    high, low = split(x)
    return jnp.concatenate([high, low, high], axis=axis)


def bdot(a, b):
    return lax.dot_general(a, b, (((1,), (0,)), ((), ())), preferred_element_type=F32)


def prepare_points(r, c, v):
    same, jmask = eye_masks()
    lane = lax.broadcasted_iota(jnp.int32, (W, W), 1)
    square = v.square
    square[...] = jnp.zeros((W, W), F32)
    square[0:8, :] = v.padded[0:8, :]
    square[ROWS_AT:ROWS_AT + 16, :] = v.padded[pl.ds(NR * r, 16), :]
    square[COLS_AT:COLS_AT + 24, :] = v.padded[pl.ds(NC * c, 24), :]
    t = square[...].T
    for i in range(NL):
        for j in range(NL):
            a_row, b_row = square[i:i + 1, :], square[j:j + 1, :]
            part = tile(kval(a_row, b_row), a_row, b_row, t[:, i:i + 1], t[:, j:j + 1], jmask)
            if i == j:
                part = part + jnp.where(same, v.noise[i:i + 1, :], 0.0)
            v.work[W * i:W * i + W, W * j:W * j + W] = part
    colp = square[COLS_AT:COLS_AT + 24, :]
    coef = []
    total = []
    for m in range(NL):
        km = kval(colp, square[m:m + 1, :])
        v.table[m, :, :] = jnp.broadcast_to(km, (24, W))
        q = -km * (unit_row() + colp - square[m:m + 1, :])
        total.append(q)
        pieces = [q if n == m else jnp.zeros((24, W), F32) for n in range(NL)]
        coef.append(jnp.concatenate(pieces, axis=1))
    weights = jnp.concatenate([jnp.concatenate(total, axis=1)] + coef + [jnp.zeros((W - 24 * (NL + 1), LEAD), F32)], axis=0)
    v.f[0:W, :] = weights
    tc = pltpu.roll(t, W - COLS_AT, 1)
    for i in range(NR):
        a_row = square[ROWS_AT + i:ROWS_AT + i + 1, :]
        a_col = t[:, ROWS_AT + i:ROWS_AT + i + 1]
        rows = slice(W * i, W * i + W)
        for l in range(NL):
            b_row = square[l:l + 1, :]
            part = tile(kval(a_row, b_row), a_row, b_row, a_col, t[:, l:l + 1], jmask)
            if l == i:
                part = part + jnp.where(same & (r == 0), v.noise[l:l + 1, :], 0.0)
            v.own[rows, W * l:W * l + W] = part
        rho = tc - a_col
        kk = jnp.exp(-0.5 * jnp.sum(rho * rho, axis=0, keepdims=True))
        v.kp[rows, :] = jnp.where((lane < NC) & ((r > 0) | (i >= NL)), kk * (unit_col() + rho), 0.0)
        alive = jnp.where(r == 0, 0.0, 1.0) if i < NL else 1.0
        v.table[NL + i, :, :] = jnp.broadcast_to(kval(colp, a_row) * alive, (24, W))
        v.h[rows, LEAD:LEAD + W] = jnp.where(jmask, -1.0, 0.0) + a_col * a_row


def factor(v, after):
    work, m_ref = v.work, v.m
    work[...] += dot_nt(v.lead[...], v.lead[...])
    for p in range(NL):
        lo, hi = W * p, W * p + W

        def write(k, x):
            m_ref[lo + 8 * k:lo + 8 * k + 8, lo:hi] = x

        invert_block(lambda k: work[lo + 8 * k:lo + 8 * k + 8, lo:hi], write)
        inv = m_ref[lo:hi, lo:hi]
        if p:
            m_ref[lo:hi, 0:lo] = dot(inv, work[lo:hi, 0:lo])
        if hi < LEAD:
            m_ref[lo:hi, hi:] = jnp.zeros((W, LEAD - hi), F32)
            u = dot(inv, work[lo:hi, hi:])
            work[hi:, hi:] -= dot_tn(u, u)
            e = dot_tn(u, m_ref[lo:hi, 0:hi])
            if p:
                work[hi:, 0:lo] -= e[:, 0:lo]
            work[hi:, lo:hi] = -e[:, lo:hi]
        after(p)
        part = m_ref[lo:hi, :]
        g = dot_tn(part, part)
        v.g[...] = g if p == 0 else v.g[...] + g
        for s in ((0, 1), (2, 3), (4,), ())[p]:
            rows = slice(2 * W * s, 2 * W * s + 2 * W)
            v.own[rows, :] += dot_nt(v.basis[rows, :], v.lead[...])


def prepare_rows(r, c, v):
    for s in range(NR // 2):
        rows = slice(2 * W * s, 2 * W * s + 2 * W)
        hs = dot(v.own[rows, :], v.g[...])
        b = v.basis[rows, :]
        if s < NL // 2:
            hs = jnp.where(r == 0, -v.m[rows, :], hs)
            b = jnp.where(r == 0, 0.0, b)
        for m in range(NL):
            v.h[rows, W * m:W * m + W] = jnp.where(lax.broadcasted_iota(jnp.int32, (2 * W, W), 1) > 0, hs[:, W * m:W * m + W], 0.0)
        eb = dot_nt(hs, v.f[...])
        v.lhs[rows, 0:3 * W] = three_left(b - eb[:, W:])
        v.lhs[rows, 3 * W:] = three_left(eb[:, 0:W] + v.kp[rows, :])

    @pl.when(c == 0)
    def _():
        for s in range(NR // 2):
            rows = slice(2 * W * s, 2 * W * s + 2 * W)
            x = dot_nt(v.own[rows, :], v.m[...])
            rid = 2 * W * s + lax.broadcasted_iota(jnp.int32, (2 * W, LEAD), 0)
            cid = lax.broadcasted_iota(jnp.int32, (2 * W, LEAD), 1)
            v.panel[rows, :] = jnp.where((r == 0) & (rid < cid), 0.0, x)


def pad_points(v, raw):
    n = raw.shape[0]
    v.padded[0:n, :] = jnp.concatenate([jnp.zeros((n, 1), F32), raw[...]], axis=1)
    v.padded[n:, :] = jnp.zeros((v.padded.shape[0] - n, W), F32)


def lead_products(v):
    v.f[W:2 * W, :] = v.lead[...].T


OUTS = (("square", (W, W), F32), ("table", (NT, 24, W), F32), ("h", (ROWS, LEAD + W), F32), ("lhs", (ROWS, 6 * W), BF),
        ("panel", (ROWS, LEAD), F32), ("noise", (NR * RG, W), F32))
WORK = (("padded", (192, W), F32), ("lead", (LEAD, W), F32), ("basis", (ROWS, W), F32),
        ("m", (LEAD, LEAD), F32), ("g", (LEAD, LEAD), F32), ("work", (LEAD, LEAD), F32), ("own", (ROWS, LEAD), F32), ("kp", (ROWS, W), F32),
        ("f", (2 * W, LEAD), F32))


def lead_kernel(points_hbm, noise_hbm, basis_hbm, *refs):
    n = len(OUTS)
    v = SimpleNamespace(**dict(zip([o[0] for o in OUTS], refs[:n])))
    cols_ref = refs[n]
    refs = refs[n + 1:]
    for spec, ref in zip(WORK, refs):
        setattr(v, spec[0], ref)
    stage, raw, in_sem, *sems = refs[len(WORK):]
    moves = Moves(basis_hbm, v.lead, stage, cols_ref, sems)
    copies = [
        pltpu.make_async_copy(points_hbm, raw, in_sem.at[0]),
        pltpu.make_async_copy(noise_hbm, v.noise, in_sem.at[1]),
        pltpu.make_async_copy(basis_hbm, v.basis, in_sem.at[2]),
    ]
    for copy in copies:
        copy.start()
    moves.barrier()
    moves.start_spread()
    for copy in copies:
        copy.wait()
    pad_points(v, raw)
    prepare_points(moves.r, moves.c, v)
    moves.finish_spread()
    moves.start_z()
    lead_products(v)

    def after(p):
        moves.forward(p)

    factor(v, after)
    prepare_rows(moves.r, moves.c, v)
    moves.finish()


def prepare(points, noise, basis):
    vmem = pl.BlockSpec(memory_space=pltpu.VMEM)
    dma = pltpu.SemaphoreType.DMA
    return pl.pallas_call(
        lead_kernel,
        out_shape=tuple(jax.ShapeDtypeStruct(o[1], o[2]) for o in OUTS) + (jax.ShapeDtypeStruct((NC * W, W), F32),),
        in_specs=[pl.BlockSpec(memory_space=pl.ANY)] * 3,
        out_specs=(vmem,) * (len(OUTS) + 1),
        scratch_shapes=[pltpu.VMEM(o[1], o[2]) for o in WORK] + [
            pltpu.VMEM((BLOCK_HALF, W), F32),
            pltpu.VMEM(points.shape, F32),
            dma((3,)),
            dma((RG,)),
            dma((RG,)),
            dma((RG,)),
            dma((2,)),
            dma((1 + 2 * CHUNKS,)),
            dma((CHUNKS, 4)),
            dma((CHUNKS,)),
            dma((CHUNKS, 4)),
            dma((2, 2, CHUNKS)),
        ],
        compiler_params=pltpu.CompilerParams(collective_id=0, has_side_effects=True, vmem_limit_bytes=32 << 20),
    )(*[pltpu.with_memory_space_constraint(a, pltpu.HBM) for a in (points, noise, basis)])


def finish_kernel(pos, square, table, h, lhs, panel, noise_ref, cols_ref, out_ref, rhs):
    r, c = pos()
    step = pl.program_id(0)
    same, _ = eye_masks()
    is_panel = (c == 0) & (step < 2)

    @pl.when(is_panel)
    def _():
        out_ref[...] = panel[:, pl.ds(pl.multiple_of(256 * jnp.minimum(step, 1), 256), 256)]

    @pl.when(jnp.logical_not(is_panel))
    def _():
        b = cols_ref[pl.ds(pl.multiple_of(256 * step, 256), 256), :]
        rhs[0:3 * W, :] = three_right(b.T, 0)
        bases = []
        row_idx = lax.broadcasted_iota(jnp.int32, (W, W), 0)
        for s in range(2):
            j = 2 * step + s
            y = square[pl.ds(COLS_AT + j, 1), :]
            ycol = jnp.sum(jnp.where(same, y, 0.0), axis=1, keepdims=True)
            bases.append(jnp.broadcast_to(unit_col() + ycol, (W, W)))
            v = jnp.where(row_idx == j, unit_row() - y, 0.0)
            for m in range(NL):
                v = v + jnp.where(row_idx == 24 + 24 * m + j, square[m:m + 1, :], 0.0)
            rhs[3 * W:, W * s:W * s + W] = three_right(v, 0)

        def rows_block(s):
            rows = slice(256 * s, 256 * s + 256)
            acc = bdot(lhs[rows, :], rhs[...])
            for ii in range(2):
                i = 2 * s + ii
                at = slice(W * i, W * i + W)
                y_i = square[ROWS_AT + i:ROWS_AT + i + 1, :]
                his = [h[at, W * m:W * m + W] for m in range(NL + 1)]
                for jj in range(2):
                    ks = [table[m, pl.ds(2 * step + jj, 1), :] for m in range(NL)]
                    ks.append(table[NL + i, pl.ds(2 * step + jj, 1), :])
                    v = acc[W * ii:W * ii + W, W * jj:W * jj + W] + bases[jj] * (ks[NL] * y_i)
                    comb = (ks[0] * his[0] + ks[1] * his[1]) + (ks[2] * his[2] + ks[3] * his[3])
                    out_ref[at, W * jj:W * jj + W] = v - (comb + ks[4] * his[4])

        for s in range(5):
            rows_block(s)

        for s in range(2):
            i = NC * c + 2 * step + s - NR * r

            @pl.when((i >= 0) & (i < NR) & ((r > 0) | (i >= NL)))
            def _():
                at = pl.ds(pl.multiple_of(W * i, W), W)
                out_ref[at, W * s:W * s + W] += jnp.where(same, noise_ref[pl.ds(NR * r + i, 1), :], 0.0)


def finish_call(pos, prepared):
    full = pl.BlockSpec(memory_space=pltpu.VMEM)
    return pl.pallas_call(
        lambda *refs: finish_kernel(pos, *refs),
        grid=(NC // 2,),
        out_shape=jax.ShapeDtypeStruct((ROWS, NC * W), F32),
        in_specs=[full] * 7,
        out_specs=pl.BlockSpec((ROWS, 2 * W), lambda s: (0, s)),
        scratch_shapes=[pltpu.VMEM((6 * W, 2 * W), BF)],
        compiler_params=pltpu.CompilerParams(vmem_limit_bytes=32 << 20),
    )(*prepared)


def body(points, noise, basis):
    prepared = prepare(points, noise, basis)

    def pos():
        return lax.axis_index("rows"), lax.axis_index("cols")

    return finish_call(pos, prepared)


def solution(mesh):
    placed = (P(), P(), P("rows", None))
    return jax.shard_map(body, mesh=mesh, in_specs=placed, out_specs=P("rows", "cols"), check_vma=False)
```

```python
from types import SimpleNamespace

import jax
import jax.numpy as jnp
from jax import lax
from jax.experimental import pallas as pl
from jax.experimental.pallas import tpu as pltpu
from jax.sharding import PartitionSpec as P

W = 128
LEAD = 512
NL = LEAD // W
NR = 10
NC = 20
RG = 16
HALF = LEAD // 2
PIECE = HALF // RG
BLOCK_HALF = NR * W // 2
CHUNKS = 4
CHUNK = BLOCK_HALF // CHUNKS
MESH = pl.DeviceIdType.MESH
HI = lax.Precision.HIGHEST
F32 = jnp.float32
BF = jnp.bfloat16


def dot(a, b):
    return lax.dot_general(a, b, (((1,), (0,)), ((), ())), precision=HI, preferred_element_type=F32)


def dot_nt(a, b):
    return lax.dot_general(a, b, (((1,), (1,)), ((), ())), precision=HI, preferred_element_type=F32)


def dot_tn(a, b):
    return lax.dot_general(a, b, (((0,), (0,)), ((), ())), precision=HI, preferred_element_type=F32)


def split(x):
    high = x.astype(BF)
    return high, (x - high.astype(F32)).astype(BF)


class Moves:
    def __init__(self, basis, lead, stage, cols, sems):
        self.basis, self.lead, self.stage, self.cols = basis, lead, stage, cols
        (self.first_sem, self.second_sem, self.lead_recv, self.half_sem, self.local_sem,
         self.a_send, self.a_recv, self.b_send, self.b_recv) = sems
        self.r = lax.axis_index("rows")
        self.c = lax.axis_index("cols")
        self.z, self.x = self.r // 4, self.r % 4
        self.y, self.k = self.c // 2, self.c % 2
        self.home = self.x // 2

    def barrier(self):
        sem = pltpu.get_barrier_semaphore()
        for off in range(1, RG):
            pl.semaphore_signal(sem, inc=1, device_id=((self.r + off) % RG, self.c), device_id_type=MESH)
        for x in range(4):
            pl.semaphore_signal(sem, inc=1, device_id=(4 * self.z + x, 2 * self.y + 1 - self.k), device_id_type=MESH)
        pl.semaphore_wait(sem, RG + 3)

    def piece(self, source, q, send_sem, target):
        rows = pl.ds(pl.multiple_of(HALF * self.k + PIECE * q, PIECE), PIECE)
        return pltpu.make_async_remote_copy(
            src_ref=source.at[rows], dst_ref=self.lead.at[rows], send_sem=send_sem, recv_sem=self.lead_recv.at[q],
            device_id=(target, self.c), device_id_type=MESH)

    def exchange(self, core):
        rows = pl.ds(pl.multiple_of(HALF * core, HALF), HALF)
        return pltpu.make_async_remote_copy(
            src_ref=self.lead.at[rows], dst_ref=self.lead.at[rows], send_sem=self.half_sem.at[0], recv_sem=self.half_sem.at[1],
            device_id=(self.r, 2 * self.y + 1 - self.k), device_id_type=MESH)

    def start_spread(self):
        @pl.when(self.r == 0)
        def _():
            for t in range(1, RG):
                self.piece(self.basis, t, self.first_sem.at[t], t).start()
            for t in range(1, RG):
                self.piece(self.basis, 0, self.second_sem.at[t], t).start()
            pltpu.make_async_copy(self.basis.at[pl.ds(0, LEAD)], self.lead, self.local_sem.at[0]).start()

        @pl.when(self.r != 0)
        def _():
            self.piece(self.lead, self.r, self.first_sem.at[0], 0).wait_recv()
            for off in range(1, RG):
                @pl.when(self.r + off != RG)
                def _():
                    self.piece(self.lead, self.r, self.second_sem.at[off], (self.r + off) % RG).start()

    def finish_spread(self):
        @pl.when(self.r == 0)
        def _():
            pltpu.make_async_copy(self.basis.at[pl.ds(0, LEAD)], self.lead, self.local_sem.at[0]).wait()
            for t in range(1, RG):
                self.piece(self.basis, t, self.first_sem.at[t], t).wait_send()
                self.piece(self.basis, 0, self.second_sem.at[t], t).wait_send()

        @pl.when(self.r != 0)
        def _():
            for off in range(1, RG):
                self.piece(self.lead, (self.r + off) % RG, self.first_sem.at[0], 0).wait_recv()
            self.exchange(self.k).start()
            self.exchange(1 - self.k).wait_recv()
            self.exchange(self.k).wait_send()
            for off in range(1, RG):
                @pl.when(self.r + off != RG)
                def _():
                    self.piece(self.lead, self.r, self.second_sem.at[off], (self.r + off) % RG).wait_send()

    def own_rows(self, n):
        return pl.ds(pl.multiple_of(BLOCK_HALF * self.k + CHUNK * n, CHUNK), CHUNK)

    def along_z(self, n, dz):
        return pltpu.make_async_remote_copy(
            src_ref=self.basis.at[self.own_rows(n)], dst_ref=self.stage.at[pl.ds(CHUNK * n, CHUNK)],
            send_sem=self.a_send.at[n, dz], recv_sem=self.a_recv.at[n],
            device_id=(4 * ((self.z + dz) % 4) + self.x, self.c), device_id_type=MESH)

    def keep(self, n):
        return pltpu.make_async_copy(self.basis.at[self.own_rows(n)], self.stage.at[pl.ds(CHUNK * n, CHUNK)], self.local_sem.at[1 + n])

    def start_z(self):
        @pl.when(self.z == self.y)
        def _():
            for n in range(CHUNKS):
                for dz in (1, 3, 2):
                    self.along_z(n, dz).start()
                self.keep(n).start()

    def place(self, block, half, n):
        return pl.ds(pl.multiple_of(2 * BLOCK_HALF * block + BLOCK_HALF * half + CHUNK * n, CHUNK), CHUNK)

    def along_x(self, n, dx):
        return pltpu.make_async_remote_copy(
            src_ref=self.stage.at[pl.ds(CHUNK * n, CHUNK)], dst_ref=self.cols.at[self.place(self.x % 2, self.k, n)],
            send_sem=self.b_send.at[n, dx], recv_sem=self.b_recv.at[self.x % 2, self.k, n],
            device_id=(4 * self.z + (self.x + dx) % 4, 2 * self.y + self.home), device_id_type=MESH)

    def settle(self, n):
        return pltpu.make_async_copy(self.stage.at[pl.ds(CHUNK * n, CHUNK)], self.cols.at[self.place(self.x % 2, self.k, n)], self.local_sem.at[1 + CHUNKS + n])

    def forward(self, n):
        @pl.when(self.z == self.y)
        def _():
            self.keep(n).wait()

        @pl.when(self.z != self.y)
        def _():
            self.along_z(n, 1).wait_recv()

        for dx in (1, 3, 2):
            self.along_x(n, dx).start()

        @pl.when(self.home == self.k)
        def _():
            self.settle(n).start()

        @pl.when(self.home != self.k)
        def _():
            self.along_x(n, 0).start()

    def finish(self):
        for n in range(CHUNKS):
            for block in range(2):
                for half in range(2):
                    mine = (self.home == self.k) & (self.x % 2 == block) & (self.k == half)

                    @pl.when(jnp.logical_not(mine))
                    def _():
                        rows = self.place(block, half, n)
                        pltpu.make_async_remote_copy(
                            src_ref=self.cols.at[rows], dst_ref=self.cols.at[rows], send_sem=self.b_send.at[n, 0],
                            recv_sem=self.b_recv.at[block, half, n],
                            device_id=(self.r, 2 * self.y + 1 - self.k), device_id_type=MESH).wait_recv()
        for n in range(CHUNKS):
            for dx in (1, 3, 2):
                self.along_x(n, dx).wait_send()

            @pl.when(self.home == self.k)
            def _():
                self.settle(n).wait()

            @pl.when(self.home != self.k)
            def _():
                self.along_x(n, 0).wait_send()

            @pl.when(self.z == self.y)
            def _():
                for dz in (1, 3, 2):
                    self.along_z(n, dz).wait_send()


def eye_masks():
    row = lax.broadcasted_iota(jnp.int32, (W, W), 0)
    col = lax.broadcasted_iota(jnp.int32, (W, W), 1)
    same = row == col
    return same, same & (col > 0)


def unit_row():
    return (lax.broadcasted_iota(jnp.int32, (1, W), 1) == 0).astype(F32)


def unit_col():
    return (lax.broadcasted_iota(jnp.int32, (W, 1), 0) == 0).astype(F32)


def kval(a_row, b_row):
    rho = a_row - b_row
    return jnp.exp(-0.5 * jnp.sum(rho * rho, axis=1, keepdims=True))


def tile(k, a_row, b_row, a_col, b_col, jmask):
    p = k * (unit_col() + b_col - a_col)
    q = unit_row() + a_row - b_row
    return jnp.where(jmask, k, 0.0) + p * q


def lane_splat(v, j):
    return jnp.broadcast_to(v[:, j:j + 1], (8, W))


def row_splat(v, j):
    return jnp.broadcast_to(v[j:j + 1, :], (8, W))


def invert_block(read, write):
    n = W // 8
    lane = lax.broadcasted_iota(jnp.int32, (8, W), 1)
    sub = lax.broadcasted_iota(jnp.int32, (8, W), 0)
    rows = {}

    def take(r):
        return rows[r] if r in rows else read(r)

    cols = [lane_splat(take(0), j) for j in range(8)]
    for k in range(n):
        own = (lane >= 8 * k) & (lane < 8 * k + 8)
        last = k + 1 == n
        if not last:
            following = take(k + 1)
            ahead = [lane_splat(following, 8 * k + j) for j in range(8)]
            below = list(ahead)
            later = [lane_splat(following, 8 * k + 8 + j) for j in range(8)]
        q = jnp.where(own, (lane - 8 * k == sub).astype(F32), take(k))
        w = scale = None
        for j in range(8):
            d = row_splat(cols[j], j)
            inv = 1.0 / d
            row_j = row_splat(q, j)
            others = jnp.where(sub == j, 0.0, cols[j])
            pivots = {j2: row_splat(cols[j2], j) for j2 in range(j + 1, 8)}
            for j2 in range(j + 1, 8):
                cols[j2] = cols[j2] - inv * (others * pivots[j2])
            q = q - inv * (others * row_j)
            w_j = row_j * lax.rsqrt(d)
            w = w_j if w is None else jnp.where(sub == j, w_j, w)
            scale = inv if scale is None else jnp.where(sub == j, inv, scale)
            if not last:
                m = below[j] * inv
                for j2 in range(j + 1, 8):
                    below[j2] = below[j2] - m * pivots[j2]
                for j2 in range(8):
                    later[j2] = later[j2] - m * row_splat(below[j], j2)
        write(k, jnp.where(lane <= 8 * k + sub, w, 0.0))
        rows.pop(k, None)
        if not last:
            q = q * scale
            qs = [row_splat(q, j) for j in range(8)]

            def update(v, c):
                t0 = c[0] * qs[0] + c[1] * qs[1]
                t1 = c[2] * qs[2] + c[3] * qs[3]
                t2 = c[4] * qs[4] + c[5] * qs[5]
                t3 = c[6] * qs[6] + c[7] * qs[7]
                return jnp.where(own, 0.0, v) - ((t0 + t1) + (t2 + t3))

            rows[k + 1] = update(following, ahead)
            cols = later
            for r in range(k + 2, n):
                v = take(r)
                rows[r] = update(v, [lane_splat(v, 8 * k + j) for j in range(8)])


ROWS_AT, COLS_AT = 8, 32
NT = NL + NR
ROWS = NR * W


def three_left(x):
    high, low = split(x)
    return jnp.concatenate([high, high, low], axis=1)


def three_right(x, axis):
    high, low = split(x)
    return jnp.concatenate([high, low, high], axis=axis)


def bdot(a, b):
    return lax.dot_general(a, b, (((1,), (0,)), ((), ())), preferred_element_type=F32)


def prepare_points(r, c, v):
    same, jmask = eye_masks()
    lane = lax.broadcasted_iota(jnp.int32, (W, W), 1)
    square = v.square
    square[...] = jnp.zeros((W, W), F32)
    square[0:8, :] = v.padded[0:8, :]
    square[ROWS_AT:ROWS_AT + 16, :] = v.padded[pl.ds(NR * r, 16), :]
    square[COLS_AT:COLS_AT + 24, :] = v.padded[pl.ds(NC * c, 24), :]
    t = square[...].T
    for i in range(NL):
        for j in range(NL):
            a_row, b_row = square[i:i + 1, :], square[j:j + 1, :]
            part = tile(kval(a_row, b_row), a_row, b_row, t[:, i:i + 1], t[:, j:j + 1], jmask)
            if i == j:
                part = part + jnp.where(same, v.noise[i:i + 1, :], 0.0)
            v.work[W * i:W * i + W, W * j:W * j + W] = part
    colp = square[COLS_AT:COLS_AT + 24, :]
    coef = []
    total = []
    for m in range(NL):
        km = kval(colp, square[m:m + 1, :])
        v.table[m, :, :] = jnp.broadcast_to(km, (24, W))
        q = -km * (unit_row() + colp - square[m:m + 1, :])
        total.append(q)
        pieces = [q if n == m else jnp.zeros((24, W), F32) for n in range(NL)]
        coef.append(jnp.concatenate(pieces, axis=1))
    weights = jnp.concatenate([jnp.concatenate(total, axis=1)] + coef + [jnp.zeros((W - 24 * (NL + 1), LEAD), F32)], axis=0)
    v.f[0:W, :] = weights
    tc = pltpu.roll(t, W - COLS_AT, 1)
    for i in range(NR):
        a_row = square[ROWS_AT + i:ROWS_AT + i + 1, :]
        a_col = t[:, ROWS_AT + i:ROWS_AT + i + 1]
        rows = slice(W * i, W * i + W)
        for l in range(NL):
            b_row = square[l:l + 1, :]
            part = tile(kval(a_row, b_row), a_row, b_row, a_col, t[:, l:l + 1], jmask)
            if l == i:
                part = part + jnp.where(same & (r == 0), v.noise[l:l + 1, :], 0.0)
            v.own[rows, W * l:W * l + W] = part
        rho = tc - a_col
        kk = jnp.exp(-0.5 * jnp.sum(rho * rho, axis=0, keepdims=True))
        v.kp[rows, :] = jnp.where((lane < NC) & ((r > 0) | (i >= NL)), kk * (unit_col() + rho), 0.0)
        alive = jnp.where(r == 0, 0.0, 1.0) if i < NL else 1.0
        v.table[NL + i, :, :] = jnp.broadcast_to(kval(colp, a_row) * alive, (24, W))
        v.h[rows, LEAD:LEAD + W] = jnp.where(jmask, -1.0, 0.0) + a_col * a_row


def factor(v, after):
    work, m_ref = v.work, v.m
    work[...] += dot_nt(v.lead[...], v.lead[...])
    for p in range(NL):
        lo, hi = W * p, W * p + W

        def write(k, x):
            m_ref[lo + 8 * k:lo + 8 * k + 8, lo:hi] = x

        invert_block(lambda k: work[lo + 8 * k:lo + 8 * k + 8, lo:hi], write)
        inv = m_ref[lo:hi, lo:hi]
        if p:
            m_ref[lo:hi, 0:lo] = dot(inv, work[lo:hi, 0:lo])
        if hi < LEAD:
            m_ref[lo:hi, hi:] = jnp.zeros((W, LEAD - hi), F32)
            u = dot(inv, work[lo:hi, hi:])
            work[hi:, hi:] -= dot_tn(u, u)
            e = dot_tn(u, m_ref[lo:hi, 0:hi])
            if p:
                work[hi:, 0:lo] -= e[:, 0:lo]
            work[hi:, lo:hi] = -e[:, lo:hi]
        after(p)
        part = m_ref[lo:hi, :]
        g = dot_tn(part, part)
        v.g[...] = g if p == 0 else v.g[...] + g
        for s in ((0, 1), (2, 3), (4,), ())[p]:
            rows = slice(2 * W * s, 2 * W * s + 2 * W)
            v.own[rows, :] += dot_nt(v.basis[rows, :], v.lead[...])


def prepare_rows(r, c, v):
    for s in range(NR // 2):
        rows = slice(2 * W * s, 2 * W * s + 2 * W)
        hs = dot(v.own[rows, :], v.g[...])
        b = v.basis[rows, :]
        if s < NL // 2:
            hs = jnp.where(r == 0, -v.m[rows, :], hs)
            b = jnp.where(r == 0, 0.0, b)
        for m in range(NL):
            v.h[rows, W * m:W * m + W] = jnp.where(lax.broadcasted_iota(jnp.int32, (2 * W, W), 1) > 0, hs[:, W * m:W * m + W], 0.0)
        eb = dot_nt(hs, v.f[...])
        v.lhs[rows, 0:3 * W] = three_left(b - eb[:, W:])
        v.lhs[rows, 3 * W:] = three_left(eb[:, 0:W] + v.kp[rows, :])

    @pl.when(c == 0)
    def _():
        for s in range(NR // 2):
            rows = slice(2 * W * s, 2 * W * s + 2 * W)
            x = jnp.concatenate([
                dot_nt(v.own[rows, 0:2 * W], v.m[0:2 * W, 0:2 * W]),
                dot_nt(v.own[rows, :], v.m[2 * W:, :]),
            ], axis=1)
            rid = 2 * W * s + lax.broadcasted_iota(jnp.int32, (2 * W, LEAD), 0)
            cid = lax.broadcasted_iota(jnp.int32, (2 * W, LEAD), 1)
            v.panel[rows, :] = jnp.where((r == 0) & (rid < cid), 0.0, x)


def pad_points(v, raw):
    n = raw.shape[0]
    v.padded[0:n, :] = jnp.concatenate([jnp.zeros((n, 1), F32), raw[...]], axis=1)
    v.padded[n:, :] = jnp.zeros((v.padded.shape[0] - n, W), F32)


def lead_products(v):
    v.f[W:2 * W, :] = v.lead[...].T


OUTS = (("square", (W, W), F32), ("table", (NT, 24, W), F32), ("h", (ROWS, LEAD + W), F32), ("lhs", (ROWS, 6 * W), BF),
        ("panel", (ROWS, LEAD), F32), ("noise", (NR * RG, W), F32))
WORK = (("padded", (192, W), F32), ("lead", (LEAD, W), F32), ("basis", (ROWS, W), F32),
        ("m", (LEAD, LEAD), F32), ("g", (LEAD, LEAD), F32), ("work", (LEAD, LEAD), F32), ("own", (ROWS, LEAD), F32), ("kp", (ROWS, W), F32),
        ("f", (2 * W, LEAD), F32))


def lead_kernel(points_hbm, noise_hbm, basis_hbm, *refs):
    n = len(OUTS)
    v = SimpleNamespace(**dict(zip([o[0] for o in OUTS], refs[:n])))
    cols_ref = refs[n]
    refs = refs[n + 1:]
    for spec, ref in zip(WORK, refs):
        setattr(v, spec[0], ref)
    stage, raw, in_sem, *sems = refs[len(WORK):]
    moves = Moves(basis_hbm, v.lead, stage, cols_ref, sems)
    copies = [
        pltpu.make_async_copy(points_hbm, raw, in_sem.at[0]),
        pltpu.make_async_copy(noise_hbm, v.noise, in_sem.at[1]),
        pltpu.make_async_copy(basis_hbm, v.basis, in_sem.at[2]),
    ]
    for copy in copies:
        copy.start()
    moves.barrier()
    moves.start_spread()
    for copy in copies:
        copy.wait()
    pad_points(v, raw)
    prepare_points(moves.r, moves.c, v)
    moves.finish_spread()
    moves.start_z()
    lead_products(v)

    def after(p):
        moves.forward(p)

    factor(v, after)
    prepare_rows(moves.r, moves.c, v)
    moves.finish()


def prepare(points, noise, basis):
    vmem = pl.BlockSpec(memory_space=pltpu.VMEM)
    dma = pltpu.SemaphoreType.DMA
    return pl.pallas_call(
        lead_kernel,
        out_shape=tuple(jax.ShapeDtypeStruct(o[1], o[2]) for o in OUTS) + (jax.ShapeDtypeStruct((NC * W, W), F32),),
        in_specs=[pl.BlockSpec(memory_space=pl.ANY)] * 3,
        out_specs=(vmem,) * (len(OUTS) + 1),
        scratch_shapes=[pltpu.VMEM(o[1], o[2]) for o in WORK] + [
            pltpu.VMEM((BLOCK_HALF, W), F32),
            pltpu.VMEM(points.shape, F32),
            dma((3,)),
            dma((RG,)),
            dma((RG,)),
            dma((RG,)),
            dma((2,)),
            dma((1 + 2 * CHUNKS,)),
            dma((CHUNKS, 4)),
            dma((CHUNKS,)),
            dma((CHUNKS, 4)),
            dma((2, 2, CHUNKS)),
        ],
        compiler_params=pltpu.CompilerParams(collective_id=0, has_side_effects=True, vmem_limit_bytes=32 << 20),
    )(*[pltpu.with_memory_space_constraint(a, pltpu.HBM) for a in (points, noise, basis)])


def finish_kernel(pos, square, table, h, lhs, panel, noise_ref, cols_ref, out_ref, rhs):
    r, c = pos()
    step = pl.program_id(0)
    same, _ = eye_masks()
    is_panel = (c == 0) & (step < 2)

    @pl.when(is_panel)
    def _():
        out_ref[...] = panel[:, pl.ds(pl.multiple_of(256 * jnp.minimum(step, 1), 256), 256)]

    @pl.when(jnp.logical_not(is_panel))
    def _():
        b = cols_ref[pl.ds(pl.multiple_of(256 * step, 256), 256), :]
        rhs[0:3 * W, :] = three_right(b.T, 0)
        bases = []
        row_idx = lax.broadcasted_iota(jnp.int32, (W, W), 0)
        for s in range(2):
            j = 2 * step + s
            y = square[pl.ds(COLS_AT + j, 1), :]
            ycol = jnp.sum(jnp.where(same, y, 0.0), axis=1, keepdims=True)
            bases.append(jnp.broadcast_to(unit_col() + ycol, (W, W)))
            v = jnp.where(row_idx == j, unit_row() - y, 0.0)
            for m in range(NL):
                v = v + jnp.where(row_idx == 24 + 24 * m + j, square[m:m + 1, :], 0.0)
            rhs[3 * W:, W * s:W * s + W] = three_right(v, 0)

        def rows_block(s):
            rows = slice(256 * s, 256 * s + 256)
            acc = bdot(lhs[rows, :], rhs[...])
            for ii in range(2):
                i = 2 * s + ii
                at = slice(W * i, W * i + W)
                y_i = square[ROWS_AT + i:ROWS_AT + i + 1, :]
                his = [h[at, W * m:W * m + W] for m in range(NL + 1)]
                for jj in range(2):
                    ks = [table[m, pl.ds(2 * step + jj, 1), :] for m in range(NL)]
                    ks.append(table[NL + i, pl.ds(2 * step + jj, 1), :])
                    v = acc[W * ii:W * ii + W, W * jj:W * jj + W] + bases[jj] * (ks[NL] * y_i)
                    comb = (ks[0] * his[0] + ks[1] * his[1]) + (ks[2] * his[2] + ks[3] * his[3])
                    out_ref[at, W * jj:W * jj + W] = v - (comb + ks[4] * his[4])

        for s in range(5):
            rows_block(s)

        for s in range(2):
            i = NC * c + 2 * step + s - NR * r

            @pl.when((i >= 0) & (i < NR) & ((r > 0) | (i >= NL)))
            def _():
                at = pl.ds(pl.multiple_of(W * i, W), W)
                out_ref[at, W * s:W * s + W] += jnp.where(same, noise_ref[pl.ds(NR * r + i, 1), :], 0.0)


def finish_call(pos, prepared):
    full = pl.BlockSpec(memory_space=pltpu.VMEM)
    return pl.pallas_call(
        lambda *refs: finish_kernel(pos, *refs),
        grid=(NC // 2,),
        out_shape=jax.ShapeDtypeStruct((ROWS, NC * W), F32),
        in_specs=[full] * 7,
        out_specs=pl.BlockSpec((ROWS, 2 * W), lambda s: (0, s)),
        scratch_shapes=[pltpu.VMEM((6 * W, 2 * W), BF)],
        compiler_params=pltpu.CompilerParams(vmem_limit_bytes=32 << 20),
    )(*prepared)


def body(points, noise, basis):
    prepared = prepare(points, noise, basis)

    def pos():
        return lax.axis_index("rows"), lax.axis_index("cols")

    return finish_call(pos, prepared)


def solution(mesh):
    placed = (P(), P(), P("rows", None))
    return jax.shard_map(body, mesh=mesh, in_specs=placed, out_specs=P("rows", "cols"), check_vma=False)
```
